32 devices in a mesh: et: 4 (over y, x), ex: 4 (over z), dp: 2 (over core).
Axes of the slice: x: 2, y: 2, z: 4, core: 2. Of those that a mesh axis runs over, the one named last changes fastest.
Arguments:
- tokens: bfloat16 [1024, 1664], P(('et', 'ex', 'dp')), may hold values from -6 to 6
- gate_probs: float32 [1024, 2], P(('et', 'ex', 'dp')), may hold values from 0.2 to 1
- expert_ids: int32 [1024, 2], P(('et', 'ex', 'dp')), may hold values from 0 to 15, as said below
- copies: int32 [16], replicated, may hold values from 1 to 2, as said below
- weight_in: bfloat16 [16, 1664, 8192], P('ex', None, ('et', 'dp')), may hold values from -0.15625 to 0.15625
- weight_out: bfloat16 [16, 8192, 1664], P('ex', ('et', 'dp')), may hold values from -0.0625 to 0.0625
- cotangent: bfloat16 [1024, 1664], P(('et', 'ex', 'dp')), may hold values from -6 to 6
Outputs:
- layer_out: bfloat16 [1024, 1664], P(('et', 'ex', 'dp'))
- grad_tokens: bfloat16 [1024, 1664], P(('et', 'ex', 'dp'))
- grad_gates: float32 [1024, 2], P(('et', 'ex', 'dp'))
- grad_weight_in: float32 [16, 1664, 8192], P('ex', None, ('et', 'dp'))
- grad_weight_out: float32 [16, 8192, 1664], P('ex', ('et', 'dp'))
The draws below stay inside these ranges and needn't reach their ends.
Inputs may be any that keep to these rules, and one draw needn't show every extreme that they name: `expert_ids`: the two experts of a token differ. Of each aligned run of 4 experts exactly one has 2 copies.
All inputs are finite; a program needn't handle non-finite values.
Results may differ from the reference program's by a relative error of at most 0.02.
Values may be sent and summed in bfloat16 or wider, within the bound.
No kernel may reach another device: no remote copies, remote signals or barrier semaphores. Data moves between devices by JAX's collectives and lax.ppermute only.
A program may use at most 192 MiB of HBM per device.

```python
import jax
import jax.numpy as jnp
from jax import lax

D = 1664
FF = 8192
EXPERTS = 16
TOP = 2
TOK_DEV = 32
CAP = 2
EXP_GRP = 4
FF_DEV = 1024
TOKENS = 1024
N_DP = 2


def pick_hot(key):
    return jax.random.randint(jax.random.fold_in(key, 9101), (), 0, EXPERTS)


def draw_copies(key, part):
    hot_id = pick_hot(key)
    group_total = EXPERTS // EXP_GRP
    chosen = jax.random.randint(jax.random.fold_in(key, 9102), (group_total,), 0, EXP_GRP)
    chosen = jnp.where(jnp.arange(group_total) == hot_id // EXP_GRP, hot_id % EXP_GRP, chosen)
    expert_range = jnp.arange(EXPERTS)
    doubled = expert_range % EXP_GRP == chosen[expert_range // EXP_GRP]
    return (1 + doubled.astype(jnp.int32)).astype(jnp.int32)


def block_pairs(key, hot_id, block_index):
    block_key = jax.random.fold_in(jax.random.fold_in(key, 9103), block_index)
    subkeys = jax.random.split(block_key, 5)
    expert_range = jnp.arange(EXPERTS)
    second = (hot_id + 1 + jax.random.randint(subkeys[0], (), 0, EXPERTS - 1)) % EXPERTS
    second_count = jax.random.randint(subkeys[1], (), 1, 2 * CAP + 1)
    random_ranks = jax.random.permutation(subkeys[2], EXPERTS)
    pushed = ((expert_range == hot_id) | (expert_range == second)).astype(jnp.int32)
    others = jnp.argsort(random_ranks + EXPERTS * pushed)
    places = jnp.arange(2 * TOK_DEV)
    cycled = others[(places - 2 * CAP - second_count) % (EXPERTS - 2)]
    labels = jnp.where(places < 2 * CAP, hot_id, jnp.where(places < 2 * CAP + second_count, second, cycled))
    labels = jnp.sort(labels)
    id_pairs = jnp.stack([labels[:TOK_DEV], labels[TOK_DEV:]], axis=1)
    id_pairs = id_pairs[jax.random.permutation(subkeys[3], TOK_DEV)]
    flip_bits = jax.random.randint(subkeys[4], (TOK_DEV, 1), 0, 2)
    return jnp.where(flip_bits == 1, id_pairs[:, ::-1], id_pairs)


def draw_expert_ids(key, part):
    hot_id = pick_hot(key)

    def one_block(block_index):
        return block_pairs(key, hot_id, block_index)
    id_pairs = jax.vmap(one_block)(jnp.arange(TOKENS // TOK_DEV))
    return id_pairs.reshape(TOKENS, 2).astype(jnp.int32)


def level_of(own_key, dims, cuts, low, high):
    def one(axis_at, shards_of):
        heights = jax.random.uniform(jax.random.fold_in(jax.random.fold_in(own_key, 6), axis_at), (shards_of,), jnp.float32, low / len(cuts), high / len(cuts))
        return jnp.repeat(jnp.exp(heights), dims[axis_at] // shards_of).reshape((-1,) + (1,) * (len(dims) - axis_at - 1))

    level = one(*cuts[0])
    for cut in cuts[1:]:
        level = level * one(*cut)
    return level


def gaussian(stream_key, dims, scale, limit, pieces=(), kind=jnp.bfloat16):
    entries = jax.random.normal(stream_key, dims, jnp.float32) * scale
    if len(pieces) > 0:
        entries = level_of(stream_key, dims, pieces, -0.22, 0.18) * entries
    return jnp.clip(entries, min=-limit, max=limit).astype(kind)


def setup_inputs(seed: int = 0) -> dict:
    splits = jax.random.split(jax.random.key(seed), 8)
    tokens = gaussian(splits[0], (TOKENS, D), 1.0, 6.0, ((0, 32),))
    gate_probs = jnp.clip(0.2 + 0.8 * jax.random.uniform(splits[1], (TOKENS, TOP), jnp.float32) ** level_of(splits[1], (TOKENS, TOP), ((0, 32),), -0.2, 0.2), 0.2, 1.0)
    expert_ids = draw_expert_ids(jax.random.fold_in(splits[7], 71), 0)
    copies = draw_copies(jax.random.fold_in(splits[7], 71), 0)
    weight_in = gaussian(splits[4], (EXPERTS, D, FF), D ** -0.5, 0.15625, ((0, 4), (2, 8)))
    weight_out = gaussian(splits[5], (EXPERTS, FF, D), FF ** -0.5, 0.0625, ((0, 4), (1, 8)))
    cotangent = gaussian(splits[6], (TOKENS, D), 1.0, 6.0, ((0, 32),))
    return dict(tokens=tokens, gate_probs=gate_probs, expert_ids=expert_ids, copies=copies, weight_in=weight_in, weight_out=weight_out, cotangent=cotangent)


gelu_scale = 0.7978845608028654


def gelu_tanh(values):
    inner_arg = gelu_scale * (values + 0.044715 * values * values * values)
    return 0.5 * values * (1.0 + jnp.tanh(inner_arg))


def gelu_slope(values):
    return jax.jvp(gelu_tanh, (values,), (jnp.ones_like(values),))[1]


def rounded(values):
    narrow = lax.optimization_barrier(values.astype(jnp.bfloat16))
    return narrow.astype(jnp.float32)


def block_table(block_ids, copies):
    flat_ids = block_ids.reshape(-1)
    labels = jnp.arange(EXPERTS, dtype=jnp.int32)
    onehot = (flat_ids[:, None] == labels[None, :]).astype(jnp.int32)
    earlier = jnp.cumsum(onehot, axis=0) - onehot
    ranking = jnp.sum(earlier * onehot, axis=1)
    allowed = CAP * jnp.sum(onehot * copies[None, :], axis=1)
    target = jnp.where(ranking < allowed, flat_ids * (2 * CAP) + ranking, -1)
    columns = jnp.arange(EXPERTS * 2 * CAP, dtype=jnp.int32)
    return (target[:, None] == columns[None, :]).astype(jnp.float32)


def one_expert(operands):
    inputs, upstream, weight_in, weight_out = operands
    portions = FF // FF_DEV
    highest = lax.Precision.HIGHEST
    flat_in = inputs.reshape(-1, D)
    flat_up = upstream.reshape(-1, D)
    pre_act = jnp.dot(flat_in, weight_in, preferred_element_type=jnp.float32)
    hidden = gelu_tanh(pre_act).astype(jnp.bfloat16)
    partials = jnp.einsum("rbf,bfd->rbd", hidden.reshape(-1, portions, FF_DEV).astype(jnp.float32),
                          weight_out.reshape(portions, FF_DEV, D).astype(jnp.float32), precision=highest)
    expert_out = jnp.sum(rounded(partials), axis=1).astype(jnp.bfloat16)
    back_hidden = jnp.dot(flat_up, weight_out.T, preferred_element_type=jnp.float32)
    slope_rows = (back_hidden * gelu_slope(pre_act)).astype(jnp.bfloat16)
    grad_parts = jnp.einsum("rbf,dbf->rbd", slope_rows.reshape(-1, portions, FF_DEV).astype(jnp.float32),
                            weight_in.reshape(D, portions, FF_DEV).astype(jnp.float32), precision=highest)
    input_grad = jnp.sum(rounded(grad_parts), axis=1).astype(jnp.bfloat16)
    replica_in = inputs.reshape(-1, N_DP, 2 * CAP, D).astype(jnp.float32)
    replica_up = upstream.reshape(-1, N_DP, 2 * CAP, D).astype(jnp.float32)
    replica_hidden = hidden.reshape(-1, N_DP, 2 * CAP, FF).astype(jnp.float32)
    replica_slope = slope_rows.reshape(-1, N_DP, 2 * CAP, FF).astype(jnp.float32)
    grad_in = jnp.sum(rounded(jnp.einsum("qrcd,qrcf->rdf", replica_in, replica_slope, precision=highest)), axis=0)
    grad_out = jnp.sum(rounded(jnp.einsum("qrcf,qrcd->rfd", replica_hidden, replica_up, precision=highest)), axis=0)
    return expert_out.reshape(inputs.shape), input_grad.reshape(inputs.shape), grad_in, grad_out


def reference(tokens, gate_probs, expert_ids, copies, weight_in, weight_out, cotangent):
    highest = lax.Precision.HIGHEST
    blocks = TOKENS // TOK_DEV

    def table_of(block_ids):
        return block_table(block_ids, copies)

    tables = jax.vmap(table_of)(expert_ids.reshape(blocks, TOK_DEV, TOP))
    token_rows = jnp.repeat(tokens, TOP, axis=0).astype(jnp.float32).reshape(blocks, TOK_DEV * TOP, D)
    upstream = (gate_probs.reshape(-1, 1) * jnp.repeat(cotangent, TOP, axis=0).astype(jnp.float32)).astype(jnp.bfloat16)
    up_rows = upstream.astype(jnp.float32).reshape(blocks, TOK_DEV * TOP, D)
    slot_in = jnp.einsum("bas,bad->bsd", tables, token_rows, precision=highest).astype(jnp.bfloat16)
    slot_up = jnp.einsum("bas,bad->bsd", tables, up_rows, precision=highest).astype(jnp.bfloat16)
    expert_in = slot_in.reshape(blocks, EXPERTS, 2 * CAP, D).transpose(1, 0, 2, 3)
    expert_up = slot_up.reshape(blocks, EXPERTS, 2 * CAP, D).transpose(1, 0, 2, 3)
    expert_out, input_grad, grad_weight_in, grad_weight_out = lax.map(
        one_expert, (expert_in, expert_up, weight_in, weight_out))
    out_slots = expert_out.transpose(1, 0, 2, 3).reshape(blocks, EXPERTS * 2 * CAP, D).astype(jnp.float32)
    assigned = jnp.einsum("bas,bsd->bad", tables, out_slots, precision=highest).reshape(TOKENS, TOP, D)
    layer_out = jnp.sum(gate_probs[:, :, None] * assigned, axis=1).astype(jnp.bfloat16)
    grad_gates = jnp.sum(cotangent.astype(jnp.float32)[:, None, :] * assigned, axis=2)
    grad_slots = input_grad.transpose(1, 0, 2, 3).reshape(blocks, EXPERTS * 2 * CAP, D).astype(jnp.float32)
    grad_assigned = jnp.einsum("bas,bsd->bad", tables, grad_slots, precision=highest).reshape(TOKENS, TOP, D)
    grad_tokens = jnp.sum(grad_assigned, axis=1).astype(jnp.bfloat16)
    return layer_out, grad_tokens, grad_gates, grad_weight_in, grad_weight_out
```

```python
import jax
import jax.numpy as jnp
from jax import lax
from jax.experimental import pallas as pl
from jax.experimental.pallas import tpu as pltpu
from jax.sharding import PartitionSpec as P


gelu_scale = 0.7978845608028654
bf16 = jnp.bfloat16
f32 = jnp.float32

ANY = pl.BlockSpec(memory_space=pl.ANY)
VMEM = pl.BlockSpec(memory_space=pltpu.VMEM)
SMEM = pl.BlockSpec(memory_space=pltpu.SMEM)


def dot(a, b):
    return lax.dot_general(a, b, (((1,), (0,)), ((), ())), preferred_element_type=f32)


def dot_nt(a, b):
    return lax.dot_general(a, b, (((1,), (1,)), ((), ())), preferred_element_type=f32)


def dot_tn(a, b):
    return lax.dot_general(a, b, (((0,), (0,)), ((), ())), preferred_element_type=f32)


def gelu_tanh(v):
    return 0.5 * v * (1.0 + jnp.tanh(gelu_scale * (v + 0.044715 * v * v * v)))


def gelu_slope(v):
    t = jnp.tanh(gelu_scale * (v + 0.044715 * v * v * v))
    inner = gelu_scale * (1.0 + 3.0 * 0.044715 * v * v)
    return 0.5 * (1.0 + t) + 0.5 * v * (1.0 - t * t) * inner


def call(body, ins, outs, scratch, specs_in, specs_out, aliases=None, name=None, limit=56):
    return pl.pallas_call(
        body,
        in_specs=specs_in,
        out_specs=specs_out,
        out_shape=outs,
        scratch_shapes=scratch,
        input_output_aliases=aliases or {},
        compiler_params=pltpu.CompilerParams(vmem_limit_bytes=limit * 2**20),
        name=name,
    )(*ins)


def shape(dims, kind):
    return jax.ShapeDtypeStruct(dims, kind)


def log2(n):
    assert n & (n - 1) == 0
    return n.bit_length() - 1


class Sizes:
    def __init__(self, tokens, weight_in, copies):
        self.et = lax.axis_size("et")
        self.ex = lax.axis_size("ex")
        self.dp = lax.axis_size("dp")
        self.tok, self.d = tokens.shape
        self.experts = copies.shape[0]
        self.gs = self.experts // self.ex
        self.f = weight_in.shape[2]
        self.cap = max(2, self.tok // 16)
        self.nb = self.gs + 1
        self.slots = self.nb * self.cap
        self.sp = -(-self.slots // 16) * 16
        self.rb = self.ex * self.cap
        self.src = self.et * self.dp
        self.rows = self.src * self.rb


def send_frame(z, tokens, gates, ids, copies, cotangent):
    def body(tok_ref, gate_ref, id_ref, copy_ref, cot_ref, *outs):
        me = lax.axis_index("ex")
        ids_v = id_ref[...]
        lab = lax.broadcasted_iota(jnp.int32, (z.tok, z.experts), 1)
        hot = [ids_v[:, k : k + 1] == lab for k in range(2)]
        count = (hot[0].astype(f32) + hot[1].astype(f32)).astype(bf16)
        row = lax.broadcasted_iota(jnp.int32, (z.tok, z.tok), 0)
        col = lax.broadcasted_iota(jnp.int32, (z.tok, z.tok), 1)
        earlier = dot((col < row).astype(f32).astype(bf16), count)
        allow = (copy_ref[...] * z.cap).astype(f32)
        columns = lax.broadcasted_iota(jnp.int32, (z.tok, z.ex * z.sp), 1)
        tables = []
        for k in range(2):
            rank = jnp.sum(jnp.where(hot[k], earlier, 0.0), axis=1, keepdims=True)
            limit = jnp.sum(jnp.where(hot[k], allow, 0.0), axis=1, keepdims=True)
            irank = rank.astype(jnp.int32)
            eid = ids_v[:, k : k + 1]
            group = (eid >> log2(z.gs)) ^ me
            within = eid & (z.gs - 1)
            slot = jnp.where(irank < z.cap, within * z.cap, (z.gs - 1) * z.cap) + irank
            target = jnp.where(rank < limit, group * z.sp + slot, -1)
            tables.append((target == columns).astype(f32).astype(bf16))
        sent = dot_tn(tables[0] + tables[1], tok_ref[...]).astype(bf16)
        cot = cot_ref[...].astype(f32)
        ups = [(gate_ref[:, k : k + 1] * cot).astype(bf16) for k in range(2)]
        sent_up = (dot_tn(tables[0], ups[0]) + dot_tn(tables[1], ups[1])).astype(bf16)
        for k in range(z.ex):
            outs[k][...] = sent[k * z.sp : (k + 1) * z.sp]
            outs[z.ex + k][...] = sent_up[k * z.sp : (k + 1) * z.sp]
        outs[2 * z.ex][...] = tables[0]
        outs[2 * z.ex + 1][...] = tables[1]

    outs = [shape((z.sp, z.d), bf16)] * (2 * z.ex) + [shape((z.tok, z.ex * z.sp), bf16)] * 2
    res = call(
        body,
        (tokens, gates, ids, copies.reshape(1, -1), cotangent),
        outs,
        [],
        [VMEM] * 5,
        [VMEM] * len(outs),
        name="send_frame",
    )
    return res[: z.ex], res[z.ex : 2 * z.ex], res[2 * z.ex :]


def block_select(z, transpose):
    dims = (z.nb * z.rb, z.ex * z.sp)
    r = lax.broadcasted_iota(jnp.int32, dims, 0)
    c = lax.broadcasted_iota(jnp.int32, dims, 1)
    block = r >> log2(z.rb)
    source = (r & (z.rb - 1)) >> log2(z.cap)
    slot = r & (z.cap - 1)
    want = source * z.sp + block * z.cap + slot
    return (want == c).astype(f32).astype(bf16)


def to_blocks(z, frames):
    def body(*refs):
        cat = jnp.concatenate([r[...] for r in refs[: z.ex]], axis=0)
        refs[z.ex][...] = dot(block_select(z, False), cat).astype(bf16)

    return call(
        body,
        frames,
        shape((z.nb * z.rb, z.d), bf16),
        [],
        [VMEM] * z.ex,
        VMEM,
        name="to_blocks",
    )


def gather_plane(z, own):
    mine = [own] + [move(own, "et", z.et, m) for m in range(1, z.et)]
    others = []
    for c in range(1, z.dp):
        others += [move(v, "dp", z.dp, c) for v in mine]
    return mine + others


def move(value, axis, size, offset):
    log2(size)
    return lax.ppermute(value, axis, [(i, i ^ offset) for i in range(size)])


def assemble(z, refs, out):
    for j in range(z.nb):
        out[j] = jnp.concatenate([r[j * z.rb : (j + 1) * z.rb, :] for r in refs], axis=0)


def scatter_rows(z, value, block, refs):
    for i, r in enumerate(refs):
        r[pl.ds(pl.multiple_of(block * z.rb, z.rb), z.rb), :] = value[i * z.rb : (i + 1) * z.rb]


def per_expert(z, copy_ref, before, work):
    base = lax.axis_index("ex") * z.gs

    def step(e, carry):
        before(e)
        doubled = copy_ref[base + e] > 1

        @pl.when(doubled)
        def _():
            work(e, (e, z.gs))

        @pl.when(jnp.logical_not(doubled))
        def _():
            work(e, (e,))

        return carry

    lax.fori_loop(0, z.gs, step, 0)


def rows_of(ref, blocks):
    if len(blocks) == 1:
        return ref[blocks[0]]
    return jnp.concatenate([ref[b] for b in blocks], axis=0)


def forward_in(z, copies, blocks, weight_in):
    def body(copy_ref, *refs):
        srcs = refs[: z.src]
        w, xall, pre, hid, buf, sem = refs[z.src :]

        def copy_of(e):
            return pltpu.make_async_copy(w.at[e], buf.at[e], sem.at[e])

        for e in range(z.gs):
            copy_of(e).start()
        assemble(z, srcs, xall)

        def work(e, ids):
            v = dot(rows_of(xall, ids), buf[e])
            h = gelu_tanh(v).astype(bf16)
            for i, b in enumerate(ids):
                pre[b] = v[i * z.rows : (i + 1) * z.rows]
                hid[b] = h[i * z.rows : (i + 1) * z.rows]

        per_expert(z, copy_ref, lambda e: copy_of(e).wait(), work)

    return call(
        body,
        (copies, *blocks, weight_in),
        [
            shape((z.nb, z.rows, z.d), bf16),
            shape((z.nb, z.rows, z.f), f32),
            shape((z.nb, z.rows, z.f), bf16),
        ],
        [pltpu.VMEM((z.gs, z.d, z.f), bf16), pltpu.SemaphoreType.DMA((z.gs,))],
        [SMEM] + [VMEM] * z.src + [ANY],
        [VMEM] * 3,
        name="forward_in",
    )


def middle(z, copies, blocks, weight_out, pre, hid):
    def body(copy_ref, *refs):
        srcs = refs[: z.src]
        w, pre_ref, hid_ref, uall, slope = refs[z.src : z.src + 5]
        outs = refs[z.src + 5 : 2 * z.src + 5]
        buf, sem = refs[2 * z.src + 5 :]

        def copy_of(e):
            return pltpu.make_async_copy(w.at[e], buf.at[e], sem.at[e])

        for e in range(z.gs):
            copy_of(e).start()
        assemble(z, srcs, uall)

        def work(e, ids):
            back = dot_nt(rows_of(uall, ids), buf[e])
            s = (back * gelu_slope(rows_of(pre_ref, ids))).astype(bf16)
            o = dot(rows_of(hid_ref, ids), buf[e]).astype(bf16)
            for i, b in enumerate(ids):
                slope[b] = s[i * z.rows : (i + 1) * z.rows]
                scatter_rows(z, o[i * z.rows : (i + 1) * z.rows], b, outs)

        per_expert(z, copy_ref, lambda e: copy_of(e).wait(), work)

    res = call(
        body,
        (copies, *blocks, weight_out, pre, hid),
        [shape((z.nb, z.rows, z.d), bf16), shape((z.nb, z.rows, z.f), bf16)]
        + [shape((z.nb * z.rb, z.d), bf16)] * z.src,
        [pltpu.VMEM((z.gs, z.f, z.d), bf16), pltpu.SemaphoreType.DMA((z.gs,))],
        [SMEM] + [VMEM] * z.src + [ANY, VMEM, VMEM],
        [VMEM] * (2 + z.src),
        name="middle",
    )
    return res[0], res[1], res[2:]


def backward_in(z, copies, slope, weight_in):
    def body(copy_ref, slope_ref, w, *refs):
        outs = refs[: z.src]
        buf, sem = refs[z.src :]

        def copy_of(e):
            return pltpu.make_async_copy(w.at[e], buf.at[e], sem.at[e])

        for e in range(z.gs):
            copy_of(e).start()

        def work(e, ids):
            g = dot_nt(rows_of(slope_ref, ids), buf[e]).astype(bf16)
            for i, b in enumerate(ids):
                scatter_rows(z, g[i * z.rows : (i + 1) * z.rows], b, outs)

        per_expert(z, copy_ref, lambda e: copy_of(e).wait(), work)

    return call(
        body,
        (copies, slope, weight_in),
        [shape((z.nb * z.rb, z.d), bf16)] * z.src,
        [pltpu.VMEM((z.gs, z.d, z.f), bf16), pltpu.SemaphoreType.DMA((z.gs,))],
        [SMEM, VMEM, ANY],
        [VMEM] * z.src,
        name="backward_in",
    )


def weight_grad(z, copies, left, right, name):
    m, n = left.shape[2], right.shape[2]
    parts = 2
    mp = m // parts

    def body(copy_ref, left_ref, right_ref, out, buf, sem):
        def copy_of(e, p):
            return pltpu.make_async_copy(
                buf.at[p], out.at[e, pl.ds(p * mp, mp), :], sem.at[p]
            )

        def before(e):
            pass

        def work(e, ids):
            r = rows_of(right_ref, ids)
            for p in range(parts):
                l = [left_ref[b, :, p * mp : (p + 1) * mp] for b in ids]
                v = dot_tn(l[0] if len(ids) == 1 else jnp.concatenate(l, axis=0), r)

                @pl.when(e > 0)
                def _():
                    copy_of(e - 1, p).wait()

                buf[p] = v
                copy_of(e, p).start()

        per_expert(z, copy_ref, before, work)
        for p in range(parts):
            copy_of(z.gs - 1, p).wait()

    return call(
        body,
        (copies, left, right),
        shape((z.gs, m, n), f32),
        [pltpu.VMEM((parts, mp, n), f32), pltpu.SemaphoreType.DMA((parts,))],
        [SMEM, VMEM, VMEM],
        ANY,
        name=name,
    )


def pair_sum(z, own, got):
    def body(*refs):
        for m in range(z.et):
            total = refs[m][...].astype(f32)
            for c in range(1, z.dp):
                total = total + refs[c * z.et + m][...].astype(f32)
            refs[z.src + m][...] = total.astype(bf16)

    return call(
        body,
        (*own, *got),
        [shape((z.nb * z.rb, z.d), bf16)] * z.et,
        [],
        [VMEM] * z.src,
        [VMEM] * z.et,
        name="pair_sum",
    )


def to_frames(z, parts):
    def body(*refs):
        total = refs[0][...].astype(f32)
        for m in range(1, z.et):
            total = total + refs[m][...].astype(f32)
        frames = dot_tn(block_select(z, True), total.astype(bf16)).astype(bf16)
        for k in range(z.ex):
            refs[z.et + k][...] = frames[k * z.sp : (k + 1) * z.sp]

    return call(
        body,
        parts,
        [shape((z.sp, z.d), bf16)] * z.ex,
        [],
        [VMEM] * z.et,
        [VMEM] * z.ex,
        name="to_frames",
    )


def settle(z, partials):
    own = list(partials[: z.et])
    got = []
    for c in range(1, z.dp):
        got += [move(v, "dp", z.dp, c) for v in partials[c * z.et : (c + 1) * z.et]]
    sums = pair_sum(z, own, got)
    parts = [sums[0]] + [move(sums[m], "et", z.et, m) for m in range(1, z.et)]
    frames = to_frames(z, parts)
    return [frames[0]] + [move(frames[k], "ex", z.ex, k) for k in range(1, z.ex)]


def combine(z, gates, cotangent, tables, outs, grads):
    def body(gate_ref, cot_ref, t0, t1, *refs):
        o = jnp.concatenate([r[...] for r in refs[: z.ex]], axis=0)
        g = jnp.concatenate([r[...] for r in refs[z.ex : 2 * z.ex]], axis=0)
        layer_ref, gtok_ref, ggate_ref = refs[2 * z.ex :]
        cot = cot_ref[...].astype(f32)
        p0 = dot(t0[...], o)
        p1 = dot(t1[...], o)
        layer_ref[...] = (gate_ref[:, 0:1] * p0 + gate_ref[:, 1:2] * p1).astype(bf16)
        s0 = jnp.sum(cot * p0, axis=1, keepdims=True)
        s1 = jnp.sum(cot * p1, axis=1, keepdims=True)
        lane = lax.broadcasted_iota(jnp.int32, (z.tok, 2), 1)
        ggate_ref[...] = jnp.where(lane == 0, s0, s1)
        gtok_ref[...] = (dot(t0[...], g) + dot(t1[...], g)).astype(bf16)

    return call(
        body,
        (gates, cotangent, *tables, *outs, *grads),
        [shape((z.tok, z.d), bf16), shape((z.tok, z.d), bf16), shape((z.tok, 2), f32)],
        [],
        [VMEM] * (4 + 2 * z.ex),
        [VMEM] * 3,
        name="combine",
    )


def shards(tokens, gate_probs, expert_ids, copies, weight_in, weight_out, cotangent):
    z = Sizes(tokens, weight_in, copies)
    frames_x, frames_u, tables = send_frame(z, tokens, gate_probs, expert_ids, copies, cotangent)
    got_x = [frames_x[0]] + [move(frames_x[k], "ex", z.ex, k) for k in range(1, z.ex)]
    got_u = [frames_u[0]] + [move(frames_u[k], "ex", z.ex, k) for k in range(1, z.ex)]
    blocks_x = gather_plane(z, to_blocks(z, got_x))
    blocks_u = gather_plane(z, to_blocks(z, got_u))
    xall, pre, hid = forward_in(z, copies, blocks_x, weight_in)
    uall, slope, out_parts = middle(z, copies, blocks_u, weight_out, pre, hid)
    grad_parts = backward_in(z, copies, slope, weight_in)
    outs = settle(z, out_parts)
    grads = settle(z, grad_parts)
    grad_weight_out = weight_grad(z, copies, hid, uall, "grad_out")
    grad_weight_in = weight_grad(z, copies, xall, slope, "grad_in")
    layer_out, grad_tokens, grad_gates = combine(z, gate_probs, cotangent, tables, outs, grads)
    return (layer_out, grad_tokens, grad_gates, grad_weight_in, grad_weight_out)


def solution(mesh):
    rows = P(("et", "ex", "dp"), None)
    w_in = P("ex", None, ("et", "dp"))
    w_out = P("ex", ("et", "dp"), None)
    return jax.shard_map(
        shards,
        mesh=mesh,
        in_specs=(rows, rows, rows, P(), w_in, w_out, rows),
        out_specs=(rows, rows, rows, w_in, w_out),
        check_vma=False,
    )
```

```python
import jax
import jax.numpy as jnp
from jax import lax
from jax.experimental import pallas as pl
from jax.experimental.pallas import tpu as pltpu
from jax.sharding import PartitionSpec as P


gelu_scale = 0.7978845608028654
bf16 = jnp.bfloat16
f32 = jnp.float32

ANY = pl.BlockSpec(memory_space=pl.ANY)
VMEM = pl.BlockSpec(memory_space=pltpu.VMEM)
SMEM = pl.BlockSpec(memory_space=pltpu.SMEM)
HBM = pl.BlockSpec(memory_space=pltpu.HBM)


def dot(a, b):
    return lax.dot_general(a, b, (((1,), (0,)), ((), ())), preferred_element_type=f32)


def dot_nt(a, b):
    return lax.dot_general(a, b, (((1,), (1,)), ((), ())), preferred_element_type=f32)


def dot_tn(a, b):
    return lax.dot_general(a, b, (((0,), (0,)), ((), ())), preferred_element_type=f32)


def gelu_tanh(v):
    return 0.5 * v * (1.0 + jnp.tanh(gelu_scale * (v + 0.044715 * v * v * v)))


def gelu_slope(v):
    t = jnp.tanh(gelu_scale * (v + 0.044715 * v * v * v))
    inner = gelu_scale * (1.0 + 3.0 * 0.044715 * v * v)
    return 0.5 * (1.0 + t) + 0.5 * v * (1.0 - t * t) * inner


def call(body, ins, outs, specs_in, specs_out, scratch=(), name=None, limit=8, cost=0):
    ins = [
        v if spec in (ANY, SMEM) else pltpu.with_memory_space_constraint(v, spec.memory_space)
        for v, spec in zip(ins, specs_in)
    ]
    return pl.pallas_call(
        body,
        in_specs=specs_in,
        out_specs=specs_out,
        out_shape=outs,
        scratch_shapes=list(scratch),
        compiler_params=pltpu.CompilerParams(vmem_limit_bytes=limit * 2**20),
        cost_estimate=pl.CostEstimate(flops=0, transcendentals=0, bytes_accessed=cost or 2**20),
        name=name,
    )(*ins)


def shape(dims, kind):
    return jax.ShapeDtypeStruct(dims, kind)


def token():
    return shape((8, 128), f32)


def log2(n):
    assert n & (n - 1) == 0
    return n.bit_length() - 1


def move(value, axis, size, offset):
    log2(size)
    return lax.ppermute(value, axis, [(i, i ^ offset) for i in range(size)])


class Sizes:
    def __init__(self, tokens, weight_in, copies):
        self.et = lax.axis_size("et")
        self.ex = lax.axis_size("ex")
        self.dp = lax.axis_size("dp")
        self.tok, self.d = tokens.shape
        self.experts = copies.shape[0]
        self.gs = self.experts // self.ex
        self.f = weight_in.shape[2]
        self.cap = max(2, self.tok // 16)
        self.nb = self.gs + 1
        self.slots = self.nb * self.cap
        self.frame = -(-2 * self.slots // 8) * 8
        self.rb = self.ex * self.cap
        self.half = self.nb * self.rb
        self.src = self.et * self.dp
        self.rows = self.src * self.rb


def diagonal(n):
    row = lax.broadcasted_iota(jnp.int32, (n, n), 0)
    return row == lax.broadcasted_iota(jnp.int32, (n, n), 1)


def as_column(row):
    return jnp.sum(jnp.where(diagonal(row.shape[1]), row, 0.0), axis=1, keepdims=True)


def as_row(column):
    return jnp.sum(jnp.where(diagonal(column.shape[0]), column, 0.0), axis=0, keepdims=True)


def stack_frames(refs):
    return jnp.concatenate([r[...].astype(f32) for r in refs], axis=0).astype(bf16)


def send_frame(z, tokens, gates, ids, copies, cotangent):
    ins = (tokens, gates, ids, copies.reshape(1, -1), cotangent)

    def body(*refs):
        n = len(ins)
        outs, held, sem = refs[n : n + z.ex + 3], refs[n + z.ex + 3 : -1], refs[-1]
        fetch = [pltpu.make_async_copy(refs[i], held[i], sem.at[i]) for i in range(n)]
        for c in fetch:
            c.start()
        for c in fetch:
            c.wait()
        tok_ref, gate_ref, id_ref, copy_ref, cot_ref = held
        me = lax.axis_index("ex")
        lab = lax.broadcasted_iota(jnp.int32, (z.experts, z.tok), 0)
        hot = [id_ref[k : k + 1, :] == lab for k in range(2)]
        count = (hot[0].astype(f32) + hot[1].astype(f32)).astype(bf16)
        row = lax.broadcasted_iota(jnp.int32, (z.tok, z.tok), 0)
        col = lax.broadcasted_iota(jnp.int32, (z.tok, z.tok), 1)
        earlier = dot(count, (row < col).astype(f32).astype(bf16))
        allow = as_column((copy_ref[...] * z.cap).astype(f32))
        places = lax.broadcasted_iota(jnp.int32, (z.ex * z.frame, z.tok), 0)
        in_tables, up_tables, ups = [], [], []
        cot = cot_ref[...].astype(f32)
        for k in range(2):
            rank = jnp.sum(jnp.where(hot[k], earlier, 0.0), axis=0, keepdims=True)
            limit = jnp.sum(jnp.where(hot[k], allow, 0.0), axis=0, keepdims=True)
            irank = rank.astype(jnp.int32)
            eid = id_ref[k : k + 1, :]
            group = (eid >> log2(z.gs)) ^ me
            within = eid & (z.gs - 1)
            slot = jnp.where(irank < z.cap, within * z.cap, (z.gs - 1) * z.cap) + irank
            target = group * z.frame + slot
            kept = rank < limit
            in_tables.append((jnp.where(kept, target, -1) == places).astype(f32).astype(bf16))
            up_tables.append(
                (jnp.where(kept, target + z.slots, -1) == places).astype(f32).astype(bf16)
            )
            ups.append((as_column(gate_ref[k : k + 1, :]) * cot).astype(bf16))
        sent = dot(in_tables[0] + in_tables[1], tok_ref[...])
        sent = sent + (dot(up_tables[0], ups[0]) + dot(up_tables[1], ups[1]))
        for k in range(z.ex):
            outs[k][...] = sent[k * z.frame : (k + 1) * z.frame].astype(bf16)
        outs[z.ex][...] = in_tables[0]
        outs[z.ex + 1][...] = in_tables[1]
        outs[z.ex + 2][...] = up_tables[0] + up_tables[1]

    outs = [shape((z.frame, z.d), bf16)] * z.ex + [shape((z.ex * z.frame, z.tok), bf16)] * 3
    res = call(
        body,
        ins,
        outs,
        [HBM] * len(ins),
        [VMEM] * len(outs),
        [pltpu.VMEM(v.shape, v.dtype) for v in ins] + [pltpu.SemaphoreType.DMA((len(ins),))],
        name="send_frame",
    )
    return res[: z.ex], res[z.ex :]


def block_select(z):
    dims = (2 * z.half, z.ex * z.frame)
    r = lax.broadcasted_iota(jnp.int32, dims, 0)
    c = lax.broadcasted_iota(jnp.int32, dims, 1)
    upper = r >= z.half
    r = jnp.where(upper, r - z.half, r)
    block = r >> log2(z.rb)
    source = (r & (z.rb - 1)) >> log2(z.cap)
    slot = r & (z.cap - 1)
    want = source * z.frame + block * z.cap + slot + jnp.where(upper, z.slots, 0)
    return (want == c).astype(f32).astype(bf16)


def to_blocks(z, frames, after):
    def body(*refs):
        rows = dot(block_select(z), stack_frames(refs[: z.ex]))
        refs[z.ex + 1][...] = rows[: z.half].astype(bf16)
        refs[z.ex + 2][...] = rows[z.half :].astype(bf16)

    return call(
        body,
        (*frames, after),
        [shape((z.half, z.d), bf16)] * 2,
        [VMEM] * z.ex + [ANY],
        [VMEM] * 2,
        name="to_blocks",
    )


def load_weights(weight, after, name):
    n = weight.shape[0]

    def body(w, _, out, mark, sem):
        copies = [pltpu.make_async_copy(w.at[e], out.at[e], sem.at[e]) for e in range(n)]
        for c in copies:
            c.start()
        mark[...] = jnp.zeros_like(mark)
        for c in copies:
            c.wait()

    return call(
        body,
        (weight, after),
        [shape(weight.shape, weight.dtype), token()],
        [HBM, ANY],
        [VMEM, VMEM],
        [pltpu.SemaphoreType.DMA((n,))],
        name=name,
        cost=2 * weight.size,
    )


def plane_moves(z, own):
    return [own] + [move(own, "et", z.et, m) for m in range(1, z.et)]


def swap_cores(z, mine, after):
    late, _ = lax.optimization_barrier((mine[1:], after))
    mine = [mine[0]] + late
    others = []
    for c in range(1, z.dp):
        others += [move(v, "dp", z.dp, c) for v in mine]
    return mine + others


def assemble(z, refs, out):
    for j in range(z.nb):
        out[j] = jnp.concatenate([r[j * z.rb : (j + 1) * z.rb, :] for r in refs], axis=0)


def scatter_rows(z, value, block, base, refs):
    start = pl.multiple_of(base + block * z.rb, 8)
    for i in range(z.src):
        refs[i // z.et][i % z.et, pl.ds(start, z.rb), :] = value[i * z.rb : (i + 1) * z.rb]


def per_expert(z, copy_ref, work):
    base = lax.axis_index("ex") * z.gs

    def step(e, carry):
        doubled = copy_ref[base + e] > 1

        @pl.when(doubled)
        def _():
            work(e, (e, z.gs))

        @pl.when(jnp.logical_not(doubled))
        def _():
            work(e, (e,))

        return carry

    lax.fori_loop(0, z.gs, step, 0)


def rows_of(ref, blocks):
    if len(blocks) == 1:
        return ref[blocks[0]]
    return jnp.concatenate([ref[b] for b in blocks], axis=0)


def forward_in(z, copies, blocks, weight_in, after):
    def body(copy_ref, *refs):
        srcs = refs[: z.src]
        w, _, xall, pre, hid, mark = refs[z.src :]
        mark[...] = jnp.zeros_like(mark)
        assemble(z, srcs, xall)

        def work(e, ids):
            v = dot(rows_of(xall, ids), w[e])
            h = gelu_tanh(v).astype(bf16)
            for i, b in enumerate(ids):
                pre[b] = v[i * z.rows : (i + 1) * z.rows]
                hid[b] = h[i * z.rows : (i + 1) * z.rows]

        per_expert(z, copy_ref, work)

    return call(
        body,
        (copies, *blocks, weight_in, after),
        [
            shape((z.nb, z.rows, z.d), bf16),
            shape((z.nb, z.rows, z.f), f32),
            shape((z.nb, z.rows, z.f), bf16),
            token(),
        ],
        [SMEM] + [VMEM] * (z.src + 2),
        [VMEM] * 4,
        name="forward_in",
        cost=16 * 2**20,
    )


def middle(z, copies, blocks, weight_in, weight_out, pre, hid):
    def body(copy_ref, *refs):
        srcs = refs[: z.src]
        win, wout, pre_ref, hid_ref, uall, slope, *outs = refs[z.src :]
        assemble(z, srcs, uall)

        def work(e, ids):
            back = dot_nt(rows_of(uall, ids), wout[e])
            s = (back * gelu_slope(rows_of(pre_ref, ids))).astype(bf16)
            o = dot(rows_of(hid_ref, ids), wout[e]).astype(bf16)
            g = dot_nt(s, win[e]).astype(bf16)
            for i, b in enumerate(ids):
                part = slice(i * z.rows, (i + 1) * z.rows)
                slope[b] = s[part]
                scatter_rows(z, o[part], b, 0, outs)
                scatter_rows(z, g[part], b, z.half, outs)

        per_expert(z, copy_ref, work)

    res = call(
        body,
        (copies, *blocks, weight_in, weight_out, pre, hid),
        [shape((z.nb, z.rows, z.d), bf16), shape((z.nb, z.rows, z.f), bf16)]
        + [shape((z.et, 2 * z.half, z.d), bf16)] * z.dp,
        [SMEM] + [VMEM] * (z.src + 4),
        [VMEM] * (2 + z.dp),
        name="middle",
        cost=48 * 2**20,
    )
    return res[0], res[1], res[2:]


def weight_grad(z, copies, left, right, after, name):
    m, n = left.shape[2], right.shape[2]
    parts = 2
    mp = m // parts

    def body(copy_ref, left_ref, right_ref, _, out, mark, buf, sem):
        mark[...] = jnp.zeros_like(mark)

        def copy_of(e, p):
            return pltpu.make_async_copy(
                buf.at[p], out.at[e, pl.ds(p * mp, mp), :], sem.at[p]
            )

        def work(e, ids):
            r = rows_of(right_ref, ids)
            for p in range(parts):
                l = [left_ref[b, :, p * mp : (p + 1) * mp] for b in ids]
                v = dot_tn(l[0] if len(ids) == 1 else jnp.concatenate(l, axis=0), r)

                @pl.when(e > 0)
                def _():
                    copy_of(e - 1, p).wait()

                buf[p] = v
                copy_of(e, p).start()

        per_expert(z, copy_ref, work)
        for p in range(parts):
            copy_of(z.gs - 1, p).wait()

    return call(
        body,
        (copies, left, right, after),
        [shape((z.gs, m, n), f32), token()],
        [SMEM, VMEM, VMEM, ANY],
        [ANY, VMEM],
        [pltpu.VMEM((parts, mp, n), f32), pltpu.SemaphoreType.DMA((parts,))],
        name=name,
        limit=16,
        cost=4 * z.gs * m * n,
    )


def pair_sum(z, own, got):
    def body(*refs):
        for m in range(z.et):
            total = refs[0][m].astype(f32)
            for c in range(1, z.dp):
                total = total + refs[c][m].astype(f32)
            refs[z.dp + m][...] = total.astype(bf16)

    return call(
        body,
        (own, *got),
        [shape((2 * z.half, z.d), bf16)] * z.et,
        [VMEM] * z.dp,
        [VMEM] * z.et,
        name="pair_sum",
    )


def to_frames(z, parts, after):
    def body(*refs):
        total = refs[0][...].astype(f32)
        for m in range(1, z.et):
            total = total + refs[m][...].astype(f32)
        frames = dot_tn(block_select(z), total.astype(bf16))
        for k in range(z.ex):
            refs[z.et + 1 + k][...] = frames[k * z.frame : (k + 1) * z.frame].astype(bf16)

    return call(
        body,
        (*parts, after),
        [shape((z.frame, z.d), bf16)] * z.ex,
        [VMEM] * z.et + [ANY],
        [VMEM] * z.ex,
        name="to_frames",
    )


def combine(z, gates, cotangent, tables, frames, after):
    def body(gate_ref, cot_ref, t0, t1, t2, *refs):
        rows = stack_frames(refs[: z.ex])
        layer_ref, gtok_ref, ggate_ref = refs[z.ex + 1 :]
        cot = cot_ref[...].astype(f32)
        p0 = dot_tn(t0[...], rows)
        p1 = dot_tn(t1[...], rows)
        gate0 = as_column(gate_ref[0:1, :])
        gate1 = as_column(gate_ref[1:2, :])
        layer_ref[...] = (gate0 * p0 + gate1 * p1).astype(bf16)
        ggate_ref[0:1, :] = as_row(jnp.sum(cot * p0, axis=1, keepdims=True))
        ggate_ref[1:2, :] = as_row(jnp.sum(cot * p1, axis=1, keepdims=True))
        gtok_ref[...] = dot_tn(t2[...], rows).astype(bf16)

    return call(
        body,
        (gates, cotangent, *tables, *frames, after),
        [shape((z.tok, z.d), bf16), shape((z.tok, z.d), bf16), shape((2, z.tok), f32)],
        [VMEM] * (5 + z.ex) + [ANY],
        [VMEM] * 3,
        name="combine",
    )


def shards(tokens, gate_probs, expert_ids, copies, weight_in, weight_out, cotangent):
    z = Sizes(tokens, weight_in, copies)
    gates = gate_probs.T
    frames, tables = send_frame(z, tokens, gates, expert_ids.T, copies, cotangent)
    got = [frames[0]] + [move(frames[k], "ex", z.ex, k) for k in range(1, z.ex)]
    win, mark = load_weights(weight_in, frames[0], "load_in")
    own_x, own_u = to_blocks(z, got, mark)
    mine_x = plane_moves(z, own_x)
    mine_u = plane_moves(z, own_u)
    wout, mark = load_weights(weight_out, own_x, "load_out")
    blocks_x = swap_cores(z, mine_x, mark)
    xall, pre, hid, mark = forward_in(z, copies, blocks_x, win, wout)
    blocks_u = swap_cores(z, mine_u, mark)
    uall, slope, parts = middle(z, copies, blocks_u, win, wout, pre, hid)
    sums = pair_sum(z, parts[0], [move(parts[c], "dp", z.dp, c) for c in range(1, z.dp)])
    parts = [sums[0]] + [move(sums[m], "et", z.et, m) for m in range(1, z.et)]
    grad_weight_out, mark = weight_grad(z, copies, hid, uall, sums[0], "grad_out")
    frames = to_frames(z, parts, mark)
    frames = [frames[0]] + [move(frames[k], "ex", z.ex, k) for k in range(1, z.ex)]
    grad_weight_in, mark = weight_grad(z, copies, xall, slope, frames[0], "grad_in")
    layer_out, grad_tokens, grad_gates = combine(z, gates, cotangent, tables, frames, mark)
    return (layer_out, grad_tokens, grad_gates.T, grad_weight_in, grad_weight_out)


def solution(mesh):
    rows = P(("et", "ex", "dp"), None)
    w_in = P("ex", None, ("et", "dp"))
    w_out = P("ex", ("et", "dp"), None)
    return jax.shard_map(
        shards,
        mesh=mesh,
        in_specs=(rows, rows, rows, P(), w_in, w_out, rows),
        out_specs=(rows, rows, rows, w_in, w_out),
        check_vma=False,
    )
```

```python
import jax
import jax.numpy as jnp
from jax import lax
from jax.experimental import pallas as pl
from jax.experimental.pallas import tpu as pltpu
from jax.sharding import PartitionSpec as P


gelu_scale = 0.7978845608028654
bf16 = jnp.bfloat16
f32 = jnp.float32

ANY = pl.BlockSpec(memory_space=pl.ANY)
VMEM = pl.BlockSpec(memory_space=pltpu.VMEM)
SMEM = pl.BlockSpec(memory_space=pltpu.SMEM)
HBM = pl.BlockSpec(memory_space=pltpu.HBM)


def dot(a, b):
    return lax.dot_general(a, b, (((1,), (0,)), ((), ())), preferred_element_type=f32)


def dot_nt(a, b):
    return lax.dot_general(a, b, (((1,), (1,)), ((), ())), preferred_element_type=f32)


def dot_tn(a, b):
    return lax.dot_general(a, b, (((0,), (0,)), ((), ())), preferred_element_type=f32)


def gelu_tanh(v):
    return 0.5 * v * (1.0 + jnp.tanh(gelu_scale * (v + 0.044715 * v * v * v)))


def gelu_slope(v):
    t = jnp.tanh(gelu_scale * (v + 0.044715 * v * v * v))
    inner = gelu_scale * (1.0 + 3.0 * 0.044715 * v * v)
    return 0.5 * (1.0 + t) + 0.5 * v * (1.0 - t * t) * inner


def call(body, ins, outs, specs_in, specs_out, scratch=(), limit=8, cost=0, aliases=None):
    ins = [
        v if any(spec is s for s in (ANY, SMEM)) else pltpu.with_memory_space_constraint(v, spec.memory_space)
        for v, spec in zip(ins, specs_in)
    ]
    return pl.pallas_call(
        body,
        in_specs=specs_in,
        out_specs=specs_out,
        out_shape=outs,
        scratch_shapes=list(scratch),
        compiler_params=pltpu.CompilerParams(vmem_limit_bytes=limit * 2**20),
        cost_estimate=pl.CostEstimate(flops=0, transcendentals=0, bytes_accessed=cost or 2**20),
        input_output_aliases=aliases or {},
    )(*ins)


def shape(dims, kind):
    return jax.ShapeDtypeStruct(dims, kind)


def token():
    return shape((8, 128), f32)


def log2(n):
    assert n & (n - 1) == 0
    return n.bit_length() - 1


def move(value, axis, size, offset):
    return lax.ppermute(value, axis, [(i, i ^ offset) for i in range(size)])


class Sizes:
    def __init__(self, tokens, weight_in, copies):
        self.et = lax.axis_size("et")
        self.ex = lax.axis_size("ex")
        self.dp = lax.axis_size("dp")
        self.tok, self.d = tokens.shape
        self.experts = copies.shape[0]
        self.gs = self.experts // self.ex
        self.f = weight_in.shape[2]
        self.cap = max(2, self.tok // 16)
        self.nb = self.gs + 1
        self.slots = self.nb * self.cap
        self.frame = -(-2 * self.slots // 8) * 8
        self.rb = self.ex * self.cap
        self.half = self.nb * self.rb
        self.src = self.et * self.dp
        self.rows = self.src * self.rb


def diagonal(n):
    row = lax.broadcasted_iota(jnp.int32, (n, n), 0)
    return row == lax.broadcasted_iota(jnp.int32, (n, n), 1)


def as_column(row):
    return jnp.sum(jnp.where(diagonal(row.shape[1]), row, 0.0), axis=1, keepdims=True)


def as_row(column):
    return jnp.sum(jnp.where(diagonal(column.shape[0]), column, 0.0), axis=0, keepdims=True)


def stack_frames(refs):
    return jnp.concatenate([r[...].astype(f32) for r in refs], axis=0).astype(bf16)


def send_frame(z, tokens, gates, ids, copies, cotangent):
    ins = (tokens, gates, ids, copies.reshape(1, -1), cotangent)

    def body(*refs):
        n = len(ins)
        outs, held, sem = refs[n : n + z.ex + 3], refs[n + z.ex + 3 : -1], refs[-1]
        fetch = [pltpu.make_async_copy(refs[i], held[i], sem.at[i]) for i in range(n)]
        for c in fetch:
            c.start()
        for c in fetch:
            c.wait()
        tok_ref, gate_ref, id_ref, copy_ref, cot_ref = held
        me = lax.axis_index("ex")
        lab = lax.broadcasted_iota(jnp.int32, (z.experts, z.tok), 0)
        hot = [id_ref[k : k + 1, :] == lab for k in range(2)]
        count = (hot[0].astype(f32) + hot[1].astype(f32)).astype(bf16)
        row = lax.broadcasted_iota(jnp.int32, (z.tok, z.tok), 0)
        col = lax.broadcasted_iota(jnp.int32, (z.tok, z.tok), 1)
        earlier = dot(count, (row < col).astype(f32).astype(bf16))
        allow = as_column((copy_ref[...] * z.cap).astype(f32))
        places = lax.broadcasted_iota(jnp.int32, (z.ex * z.frame, z.tok), 0)
        in_tables, up_tables, ups = [], [], []
        cot = cot_ref[...].astype(f32)
        for k in range(2):
            rank = jnp.sum(jnp.where(hot[k], earlier, 0.0), axis=0, keepdims=True)
            limit = jnp.sum(jnp.where(hot[k], allow, 0.0), axis=0, keepdims=True)
            irank = rank.astype(jnp.int32)
            eid = id_ref[k : k + 1, :]
            group = (eid >> log2(z.gs)) ^ me
            within = eid & (z.gs - 1)
            slot = jnp.where(irank < z.cap, within * z.cap, (z.gs - 1) * z.cap) + irank
            target = group * z.frame + slot
            kept = rank < limit
            in_tables.append((jnp.where(kept, target, -1) == places).astype(f32).astype(bf16))
            up_tables.append(
                (jnp.where(kept, target + z.slots, -1) == places).astype(f32).astype(bf16)
            )
            ups.append((as_column(gate_ref[k : k + 1, :]) * cot).astype(bf16))
        sent = dot(in_tables[0] + in_tables[1], tok_ref[...])
        sent = sent + (dot(up_tables[0], ups[0]) + dot(up_tables[1], ups[1]))
        for k in range(z.ex):
            outs[k][...] = sent[k * z.frame : (k + 1) * z.frame].astype(bf16)
        outs[z.ex][...] = in_tables[0]
        outs[z.ex + 1][...] = in_tables[1]
        outs[z.ex + 2][...] = up_tables[0] + up_tables[1]

    outs = [shape((z.frame, z.d), bf16)] * z.ex + [shape((z.ex * z.frame, z.tok), bf16)] * 3
    res = call(
        body,
        ins,
        outs,
        [HBM] * len(ins),
        [VMEM] * len(outs),
        [pltpu.VMEM(v.shape, v.dtype) for v in ins] + [pltpu.SemaphoreType.DMA((len(ins),))],
    )
    return res[: z.ex], res[z.ex :]


def block_select(z):
    dims = (2 * z.half, z.ex * z.frame)
    r = lax.broadcasted_iota(jnp.int32, dims, 0)
    c = lax.broadcasted_iota(jnp.int32, dims, 1)
    upper = r >= z.half
    r = jnp.where(upper, r - z.half, r)
    block = r >> log2(z.rb)
    source = (r & (z.rb - 1)) >> log2(z.cap)
    slot = r & (z.cap - 1)
    want = source * z.frame + block * z.cap + slot + jnp.where(upper, z.slots, 0)
    return (want == c).astype(f32).astype(bf16)


def to_blocks(z, frames, after):
    def body(*refs):
        rows = dot(block_select(z), stack_frames(refs[: z.ex]))
        refs[z.ex + 1][...] = rows[: z.half].astype(bf16)
        refs[z.ex + 2][...] = rows[z.half :].astype(bf16)

    return call(
        body, (*frames, after), [shape((z.half, z.d), bf16)] * 2, [VMEM] * z.ex + [ANY], [VMEM] * 2
    )


def load_weights(weight, after):
    n = weight.shape[0]

    def body(w, _, out, mark, sem):
        copies = [pltpu.make_async_copy(w.at[e], out.at[e], sem.at[e]) for e in range(n)]
        for c in copies:
            c.start()
        mark[...] = jnp.zeros_like(mark)
        for c in copies:
            c.wait()

    return call(
        body,
        (weight, after),
        [shape(weight.shape, weight.dtype), token()],
        [HBM, ANY],
        [VMEM, VMEM],
        [pltpu.SemaphoreType.DMA((n,))],
        cost=2 * weight.size,
    )


def plane_moves(z, own):
    return [own] + [move(own, "et", z.et, m) for m in range(1, z.et)]


def swap_cores(z, mine, after):
    late, _ = lax.optimization_barrier((mine[1:], after))
    mine = [mine[0]] + late
    others = []
    for c in range(1, z.dp):
        others += [move(v, "dp", z.dp, c) for v in mine]
    return mine + others


def assemble(z, refs, out):
    for j in range(z.nb):
        out[j] = jnp.concatenate([r[j * z.rb : (j + 1) * z.rb, :] for r in refs], axis=0)


def scatter_rows(z, value, block, base, refs):
    start = pl.multiple_of(base + block * z.rb, 8)
    for i in range(z.src):
        refs[i // z.et][i % z.et, pl.ds(start, z.rb), :] = value[i * z.rb : (i + 1) * z.rb]


def per_expert(z, copy_ref, work):
    base = lax.axis_index("ex") * z.gs

    def step(e, carry):
        doubled = copy_ref[base + e] > 1

        @pl.when(doubled)
        def _():
            work(e, (e, z.gs))

        @pl.when(jnp.logical_not(doubled))
        def _():
            work(e, (e,))

        return carry

    lax.fori_loop(0, z.gs, step, 0)


def rows_of(ref, blocks):
    if len(blocks) == 1:
        return ref[blocks[0]]
    return jnp.concatenate([ref[b] for b in blocks], axis=0)


def forward_in(z, copies, blocks, weight_in, after):
    def body(copy_ref, *refs):
        srcs = refs[: z.src]
        w, _, xall, pre, hid, mark = refs[z.src :]
        mark[...] = jnp.zeros_like(mark)
        assemble(z, srcs, xall)

        def work(e, ids):
            v = dot(rows_of(xall, ids), w[e])
            h = gelu_tanh(v).astype(bf16)
            for i, b in enumerate(ids):
                pre[b] = v[i * z.rows : (i + 1) * z.rows]
                hid[b] = h[i * z.rows : (i + 1) * z.rows]

        per_expert(z, copy_ref, work)

    return call(
        body,
        (copies, *blocks, weight_in, after),
        [
            shape((z.nb, z.rows, z.d), bf16),
            shape((z.nb, z.rows, z.f), f32),
            shape((z.nb, z.rows, z.f), bf16),
            token(),
        ],
        [SMEM] + [VMEM] * (z.src + 2),
        [VMEM] * 4,
        cost=16 * 2**20,
    )


def middle(z, copies, blocks, weight_in, weight_out, pre, hid):
    def body(copy_ref, *refs):
        srcs = refs[: z.src]
        win, wout, pre_ref, hid_ref, uall, slope, *outs = refs[z.src :]
        assemble(z, srcs, uall)

        def work(e, ids):
            back = dot_nt(rows_of(uall, ids), wout[e])
            s = (back * gelu_slope(rows_of(pre_ref, ids))).astype(bf16)
            o = dot(rows_of(hid_ref, ids), wout[e]).astype(bf16)
            g = dot_nt(s, win[e]).astype(bf16)
            for i, b in enumerate(ids):
                part = slice(i * z.rows, (i + 1) * z.rows)
                slope[b] = s[part]
                scatter_rows(z, o[part], b, 0, outs)
                scatter_rows(z, g[part], b, z.half, outs)

        per_expert(z, copy_ref, work)

    res = call(
        body,
        (copies, *blocks, weight_in, weight_out, pre, hid),
        [shape((z.nb, z.rows, z.d), bf16), shape((z.nb, z.rows, z.f), bf16)]
        + [shape((z.et, 2 * z.half, z.d), bf16)] * z.dp,
        [SMEM] + [VMEM] * (z.src + 4),
        [VMEM] * (2 + z.dp),
        cost=48 * 2**20,
    )
    return res[0], res[1], res[2:]


def weight_grads(z, copies, rows, jobs, held, after):
    kinds = [which for which, _, _ in jobs]
    operands, spans, alias = [], [], {}
    for which in kinds:
        operands += list(rows[which])
    for which in kinds:
        tiles = rows[which][0].shape[2] // 128
        edge = (tiles + 1) // 2 * 128
        spans.append(((0, edge), (edge, tiles * 128 - edge)))
    parts = 2
    old = [held[which] for which in kinds if held[which] is not None]
    at = 1 + len(operands)
    for i, which in enumerate(kinds):
        if held[which] is not None:
            alias[at] = i
            at += 1

    def body(copy_ref, *refs):
        ins = refs[: len(operands)]
        outs = refs[len(operands) + len(old) + 1 :]
        mark = outs[len(jobs)]
        sems = outs[-1]
        mark[...] = jnp.zeros_like(mark)
        base = lax.axis_index("ex") * z.gs

        def copy_of(i, e, p):
            start, size = spans[i][p]
            src = outs[len(jobs) + 1 + i].at[pl.ds(start, size), :]
            return pltpu.make_async_copy(src, outs[i].at[e, pl.ds(start, size), :], sems.at[i, p])

        def work(i, first, e, ids):
            left, right = ins[2 * i], ins[2 * i + 1]
            buf = outs[len(jobs) + 1 + i]
            r = rows_of(right, ids)
            for p, (start, size) in enumerate(spans[i]):
                l = [left[b, :, start : start + size] for b in ids]
                v = dot_tn(l[0] if len(ids) == 1 else jnp.concatenate(l, axis=0), r)

                @pl.when(e > first)
                def _():
                    copy_of(i, e - 1, p).wait()

                buf[start : start + size, :] = v
                copy_of(i, e, p).start()

        for i, (which, first, last) in enumerate(jobs):

            def step(e, carry):
                doubled = copy_ref[base + e] > 1

                @pl.when(doubled)
                def _():
                    work(i, first, e, (e, z.gs))

                @pl.when(jnp.logical_not(doubled))
                def _():
                    work(i, first, e, (e,))

                return carry

            lax.fori_loop(first, last, step, 0)
        for i, (which, first, last) in enumerate(jobs):
            for p in range(parts):
                copy_of(i, last - 1, p).wait()

    outs = [
        pltpu.HBM((z.gs, rows[which][0].shape[2], rows[which][1].shape[2]), f32)
        for which in kinds
    ]
    res = call(
        body,
        (copies, *operands, *old, after),
        outs + [token()],
        [SMEM] + [VMEM] * len(operands) + [HBM] * len(old) + [ANY],
        [HBM] * len(jobs) + [VMEM],
        [pltpu.VMEM((rows[w][0].shape[2], rows[w][1].shape[2]), f32) for w in kinds]
        + [pltpu.SemaphoreType.DMA((len(jobs), parts))],
        limit=24,
        cost=4 * sum((last - first) * rows[w][0].shape[2] * rows[w][1].shape[2] for w, first, last in jobs),
        aliases=alias,
    )
    held = list(held)
    for i, which in enumerate(kinds):
        held[which] = res[i]
    return held, res[-1]


def pair_sum(z, own, got, after):
    def body(*refs):
        for m in range(z.et):
            total = refs[0][m].astype(f32)
            for c in range(1, z.dp):
                total = total + refs[c][m].astype(f32)
            refs[z.dp + 1 + m][...] = total.astype(bf16)

    return call(
        body,
        (own, *got, after),
        [shape((2 * z.half, z.d), bf16)] * z.et,
        [VMEM] * z.dp + [ANY],
        [VMEM] * z.et,
    )


def to_frames(z, parts, after):
    def body(*refs):
        total = refs[0][...].astype(f32)
        for m in range(1, z.et):
            total = total + refs[m][...].astype(f32)
        frames = dot_tn(block_select(z), total.astype(bf16))
        for k in range(z.ex):
            refs[z.et + 1 + k][...] = frames[k * z.frame : (k + 1) * z.frame].astype(bf16)

    return call(
        body,
        (*parts, after),
        [shape((z.frame, z.d), bf16)] * z.ex,
        [VMEM] * z.et + [ANY],
        [VMEM] * z.ex,
    )


def combine(z, gates, cotangent, tables, frames, after):
    def body(gate_ref, cot_ref, t0, t1, t2, *refs):
        rows = stack_frames(refs[: z.ex])
        layer_ref, gtok_ref, ggate_ref = refs[z.ex + 1 :]
        cot = cot_ref[...].astype(f32)
        p0 = dot_tn(t0[...], rows)
        p1 = dot_tn(t1[...], rows)
        gate0 = as_column(gate_ref[0:1, :])
        gate1 = as_column(gate_ref[1:2, :])
        layer_ref[...] = (gate0 * p0 + gate1 * p1).astype(bf16)
        ggate_ref[0:1, :] = as_row(jnp.sum(cot * p0, axis=1, keepdims=True))
        ggate_ref[1:2, :] = as_row(jnp.sum(cot * p1, axis=1, keepdims=True))
        gtok_ref[...] = dot_tn(t2[...], rows).astype(bf16)

    return call(
        body,
        (gates, cotangent, *tables, *frames, after),
        [shape((z.tok, z.d), bf16), shape((z.tok, z.d), bf16), shape((2, z.tok), f32)],
        [VMEM] * (5 + z.ex) + [ANY],
        [VMEM] * 3,
    )


def shards(tokens, gate_probs, expert_ids, copies, weight_in, weight_out, cotangent):
    z = Sizes(tokens, weight_in, copies)
    gates = gate_probs.T
    frames, tables = send_frame(z, tokens, gates, expert_ids.T, copies, cotangent)
    got = [frames[0]] + [move(frames[k], "ex", z.ex, k) for k in range(1, z.ex)]
    win, mark = load_weights(weight_in, frames[0])
    own_x, own_u = to_blocks(z, got, mark)
    mine_x = plane_moves(z, own_x)
    mine_u = plane_moves(z, own_u)
    wout, mark = load_weights(weight_out, own_x)
    blocks_x = swap_cores(z, mine_x, mark)
    xall, pre, hid, mark = forward_in(z, copies, blocks_x, win, wout)
    blocks_u = swap_cores(z, mine_u, mark)
    uall, slope, parts = middle(z, copies, blocks_u, win, wout, pre, hid)
    pairs = ((hid, uall), (xall, slope))
    held = [None, None]
    swapped = [move(parts[c], "dp", z.dp, c) for c in range(1, z.dp)]
    held, mark = weight_grads(z, copies, pairs, [(0, 0, 1)], held, parts[1])
    sums = pair_sum(z, parts[0], swapped, mark)
    parts = [sums[0]] + [move(sums[m], "et", z.et, m) for m in range(1, z.et)]
    held, mark = weight_grads(z, copies, pairs, [(0, 1, z.gs), (1, 0, 1)], held, sums[0])
    frames = to_frames(z, parts, mark)
    frames = [frames[0]] + [move(frames[k], "ex", z.ex, k) for k in range(1, z.ex)]
    held, mark = weight_grads(z, copies, pairs, [(1, 1, z.gs)], held, frames[0])
    grad_weight_out, grad_weight_in = held
    layer_out, grad_tokens, grad_gates = combine(z, gates, cotangent, tables, frames, mark)
    return (layer_out, grad_tokens, grad_gates.T, grad_weight_in, grad_weight_out)


def solution(mesh):
    rows = P(("et", "ex", "dp"), None)
    w_in = P("ex", None, ("et", "dp"))
    w_out = P("ex", ("et", "dp"), None)
    return jax.shard_map(
        shards,
        mesh=mesh,
        in_specs=(rows, rows, rows, P(), w_in, w_out, rows),
        out_specs=(rows, rows, rows, w_in, w_out),
        check_vma=False,
    )
```

```python
import jax
import jax.numpy as jnp
from jax import lax
from jax.experimental import pallas as pl
from jax.experimental.pallas import tpu as pltpu
from jax.sharding import PartitionSpec as P


gelu_scale = 0.7978845608028654
bf16 = jnp.bfloat16
f32 = jnp.float32

ANY = pl.BlockSpec(memory_space=pl.ANY)
VMEM = pl.BlockSpec(memory_space=pltpu.VMEM)
SMEM = pl.BlockSpec(memory_space=pltpu.SMEM)
HBM = pl.BlockSpec(memory_space=pltpu.HBM)


def dot(a, b):
    return lax.dot_general(a, b, (((1,), (0,)), ((), ())), preferred_element_type=f32)


def dot_nt(a, b):
    return lax.dot_general(a, b, (((1,), (1,)), ((), ())), preferred_element_type=f32)


def dot_tn(a, b):
    return lax.dot_general(a, b, (((0,), (0,)), ((), ())), preferred_element_type=f32)


def gelu_tanh(v):
    return 0.5 * v * (1.0 + jnp.tanh(gelu_scale * (v + 0.044715 * v * v * v)))


def gelu_slope(v):
    t = jnp.tanh(gelu_scale * (v + 0.044715 * v * v * v))
    inner = gelu_scale * (1.0 + 3.0 * 0.044715 * v * v)
    return 0.5 * (1.0 + t) + 0.5 * v * (1.0 - t * t) * inner


def call(body, ins, outs, specs_in, specs_out, scratch=(), limit=8, cost=0, aliases=None):
    ins = [
        v if any(spec is s for s in (ANY, SMEM)) else pltpu.with_memory_space_constraint(v, spec.memory_space)
        for v, spec in zip(ins, specs_in)
    ]
    return pl.pallas_call(
        body,
        in_specs=specs_in,
        out_specs=specs_out,
        out_shape=outs,
        scratch_shapes=list(scratch),
        compiler_params=pltpu.CompilerParams(vmem_limit_bytes=limit * 2**20),
        cost_estimate=pl.CostEstimate(flops=0, transcendentals=0, bytes_accessed=cost or 2**20),
        input_output_aliases=aliases or {},
    )(*ins)


def shape(dims, kind):
    return jax.ShapeDtypeStruct(dims, kind)


def token():
    return shape((8, 128), f32)


def log2(n):
    assert n & (n - 1) == 0
    return n.bit_length() - 1


def move(value, axis, size, offset):
    return lax.ppermute(value, axis, [(i, i ^ offset) for i in range(size)])


class Sizes:
    def __init__(self, tokens, weight_in, copies):
        self.et = lax.axis_size("et")
        self.ex = lax.axis_size("ex")
        self.dp = lax.axis_size("dp")
        self.tok, self.d = tokens.shape
        self.experts = copies.shape[0]
        self.gs = self.experts // self.ex
        self.f = weight_in.shape[2]
        self.cap = max(2, self.tok // 16)
        self.nb = self.gs + 1
        self.slots = self.nb * self.cap
        self.frame = -(-2 * self.slots // 8) * 8
        self.rb = self.ex * self.cap
        self.half = self.nb * self.rb
        self.src = self.et * self.dp
        self.rows = self.src * self.rb


def diagonal(n):
    row = lax.broadcasted_iota(jnp.int32, (n, n), 0)
    return row == lax.broadcasted_iota(jnp.int32, (n, n), 1)


def as_column(row):
    return jnp.sum(jnp.where(diagonal(row.shape[1]), row, 0.0), axis=1, keepdims=True)


def as_row(column):
    return jnp.sum(jnp.where(diagonal(column.shape[0]), column, 0.0), axis=0, keepdims=True)


def stack_frames(refs):
    return jnp.concatenate([r[...].astype(f32) for r in refs], axis=0).astype(bf16)


def send_frame(z, tokens, gates, ids, copies, cotangent):
    ins = (tokens, gates, ids, copies.reshape(1, -1), cotangent)

    def body(*refs):
        n = len(ins)
        outs, held, sem = refs[n : n + z.ex + 3], refs[n + z.ex + 3 : -1], refs[-1]
        fetch = [pltpu.make_async_copy(refs[i], held[i], sem.at[i]) for i in range(n)]
        for c in fetch:
            c.start()
        for c in fetch:
            c.wait()
        tok_ref, gate_ref, id_ref, copy_ref, cot_ref = held
        me = lax.axis_index("ex")
        lab = lax.broadcasted_iota(jnp.int32, (z.experts, z.tok), 0)
        hot = [id_ref[k : k + 1, :] == lab for k in range(2)]
        count = (hot[0].astype(f32) + hot[1].astype(f32)).astype(bf16)
        row = lax.broadcasted_iota(jnp.int32, (z.tok, z.tok), 0)
        col = lax.broadcasted_iota(jnp.int32, (z.tok, z.tok), 1)
        earlier = dot(count, (row < col).astype(f32).astype(bf16))
        allow = as_column((copy_ref[...] * z.cap).astype(f32))
        places = lax.broadcasted_iota(jnp.int32, (z.ex * z.frame, z.tok), 0)
        in_tables, up_tables, ups = [], [], []
        cot = cot_ref[...].astype(f32)
        for k in range(2):
            rank = jnp.sum(jnp.where(hot[k], earlier, 0.0), axis=0, keepdims=True)
            limit = jnp.sum(jnp.where(hot[k], allow, 0.0), axis=0, keepdims=True)
            irank = rank.astype(jnp.int32)
            eid = id_ref[k : k + 1, :]
            group = (eid >> log2(z.gs)) ^ me
            within = eid & (z.gs - 1)
            slot = jnp.where(irank < z.cap, within * z.cap, (z.gs - 1) * z.cap) + irank
            target = group * z.frame + slot
            kept = rank < limit
            in_tables.append((jnp.where(kept, target, -1) == places).astype(f32).astype(bf16))
            up_tables.append(
                (jnp.where(kept, target + z.slots, -1) == places).astype(f32).astype(bf16)
            )
            ups.append((as_column(gate_ref[k : k + 1, :]) * cot).astype(bf16))
        sent = dot(in_tables[0] + in_tables[1], tok_ref[...])
        sent = sent + (dot(up_tables[0], ups[0]) + dot(up_tables[1], ups[1]))
        for k in range(z.ex):
            outs[k][...] = sent[k * z.frame : (k + 1) * z.frame].astype(bf16)
        outs[z.ex][...] = in_tables[0]
        outs[z.ex + 1][...] = in_tables[1]
        outs[z.ex + 2][...] = up_tables[0] + up_tables[1]

    outs = [shape((z.frame, z.d), bf16)] * z.ex + [shape((z.ex * z.frame, z.tok), bf16)] * 3
    res = call(
        body,
        ins,
        outs,
        [HBM] * len(ins),
        [VMEM] * len(outs),
        [pltpu.VMEM(v.shape, v.dtype) for v in ins] + [pltpu.SemaphoreType.DMA((len(ins),))],
    )
    return res[: z.ex], res[z.ex :]


def block_select(z):
    dims = (2 * z.half, z.ex * z.frame)
    r = lax.broadcasted_iota(jnp.int32, dims, 0)
    c = lax.broadcasted_iota(jnp.int32, dims, 1)
    upper = r >= z.half
    r = jnp.where(upper, r - z.half, r)
    block = r >> log2(z.rb)
    source = (r & (z.rb - 1)) >> log2(z.cap)
    slot = r & (z.cap - 1)
    want = source * z.frame + block * z.cap + slot + jnp.where(upper, z.slots, 0)
    return (want == c).astype(f32).astype(bf16)


def frame_moves(z, frames):
    moved = []
    for k in range(1, z.ex):
        moved.append(move(frames[k], "ex", z.ex, k))
    return [frames[0]] + moved


def to_blocks(z, frames, after):
    def body(*refs):
        rows = dot(block_select(z), stack_frames(refs[: z.ex]))
        refs[z.ex + 1][...] = rows[: z.half].astype(bf16)
        refs[z.ex + 2][...] = rows[z.half :].astype(bf16)

    return call(
        body, (*frames, after), [shape((z.half, z.d), bf16)] * 2, [VMEM] * z.ex + [ANY], [VMEM] * 2
    )


def load_weights(weight, after, n):
    dims = (n,) + weight.shape[1:]

    def body(w, _, out, mark, sem):
        copies = [pltpu.make_async_copy(w.at[e], out.at[e], sem.at[e]) for e in range(n)]
        for c in copies:
            c.start()
        mark[...] = jnp.zeros_like(mark)
        for c in copies:
            c.wait()

    return call(
        body,
        (weight, after),
        [shape(dims, weight.dtype), token()],
        [HBM, ANY],
        [VMEM, VMEM],
        [pltpu.SemaphoreType.DMA((n,))],
        cost=2 * weight.size // weight.shape[0] * n,
    )


def plane_moves(z, own):
    return [own] + [move(own, "et", z.et, m) for m in range(1, z.et)]


def swap_cores(z, mine, after):
    late, _ = lax.optimization_barrier((mine[1:], after))
    mine = [mine[0]] + late
    others = []
    for c in range(1, z.dp):
        others.append(move(mine[0], "dp", z.dp, c))
        others += [move(v, "dp", z.dp, c) for v in mine[1:]]
    return mine + others


def assemble(z, refs, out):
    for j in range(z.nb):
        out[j] = jnp.concatenate([r[j * z.rb : (j + 1) * z.rb, :] for r in refs], axis=0)


def scatter_rows(z, value, block, base, refs):
    start = pl.multiple_of(base + block * z.rb, 8)
    for i in range(z.src):
        refs[i // z.et][i % z.et, pl.ds(start, z.rb), :] = value[i * z.rb : (i + 1) * z.rb]


def per_expert(z, copy_ref, work, first=0, last=None):
    base = lax.axis_index("ex") * z.gs

    def step(e, carry):
        doubled = copy_ref[base + e] > 1

        @pl.when(doubled)
        def _():
            work(e, (e, z.gs))

        @pl.when(jnp.logical_not(doubled))
        def _():
            work(e, (e,))

        return carry

    lax.fori_loop(first, z.gs if last is None else last, step, 0)


def rows_of(ref, blocks):
    if len(blocks) == 1:
        return ref[blocks[0]]
    return jnp.concatenate([ref[b] for b in blocks], axis=0)


def forward_in(z, copies, blocks, weight_in, after):
    def body(copy_ref, *refs):
        srcs = refs[: z.src]
        w, _, xall, pre, hid, mark = refs[z.src :]
        mark[...] = jnp.zeros_like(mark)
        assemble(z, srcs, xall)

        def work(e, ids):
            v = dot(rows_of(xall, ids), w[e])
            h = gelu_tanh(v).astype(bf16)
            for i, b in enumerate(ids):
                pre[b] = v[i * z.rows : (i + 1) * z.rows]
                hid[b] = h[i * z.rows : (i + 1) * z.rows]

        per_expert(z, copy_ref, work)

    return call(
        body,
        (copies, *blocks, weight_in, after),
        [
            shape((z.nb, z.rows, z.d), bf16),
            shape((z.nb, z.rows, z.f), f32),
            shape((z.nb, z.rows, z.f), bf16),
            token(),
        ],
        [SMEM] + [VMEM] * (z.src + 2),
        [VMEM] * 4,
        cost=16 * 2**20,
    )


def middle(z, copies, blocks, weight_in, ready, weight_out, pre, hid, early):
    done = ready.shape[0]

    def body(copy_ref, *refs):
        srcs = refs[: z.src]
        win, wout, whbm, pre_ref, hid_ref, uall, slope, *outs = refs[z.src :]
        *outs, grad, buf, sem, wrest, wsem = outs
        fetch = [
            pltpu.make_async_copy(whbm.at[e], wrest.at[e - done], wsem.at[e - done])
            for e in range(done, z.gs)
        ]
        for c in fetch:
            c.start()
        assemble(z, srcs, uall)

        def write(e):
            return pltpu.make_async_copy(buf, grad.at[e], sem)

        def work(e, ids, last=False):
            w = wrest[e - done] if last else wout[e]
            back = dot_nt(rows_of(uall, ids), w)
            s = (back * gelu_slope(rows_of(pre_ref, ids))).astype(bf16)
            o = dot(rows_of(hid_ref, ids), w).astype(bf16)
            g = dot_nt(s, win[e]).astype(bf16)
            for i, b in enumerate(ids):
                part = slice(i * z.rows, (i + 1) * z.rows)
                slope[b] = s[part]
                scatter_rows(z, o[part], b, 0, outs)
                scatter_rows(z, g[part], b, z.half, outs)

        def early_work(e, ids):
            work(e, ids)

            @pl.when(e > 0)
            def _():
                write(e - 1).wait()

            r = rows_of(uall, ids)
            for i in range(z.f // 128):
                part = slice(i * 128, (i + 1) * 128)
                l = [hid_ref[b, :, part] for b in ids]
                buf[part, :] = dot_tn(l[0] if len(ids) == 1 else jnp.concatenate(l, axis=0), r)
            write(e).start()

        per_expert(z, copy_ref, early_work, 0, early)
        per_expert(z, copy_ref, work, early, done)
        for c in fetch:
            c.wait()
        per_expert(z, copy_ref, lambda e, ids: work(e, ids, True), done, z.gs)
        write(early - 1).wait()

    res = call(
        body,
        (copies, *blocks, weight_in, ready, weight_out, pre, hid),
        [shape((z.nb, z.rows, z.d), bf16), shape((z.nb, z.rows, z.f), bf16)]
        + [shape((z.et, 2 * z.half, z.d), bf16)] * z.dp
        + [pltpu.HBM((z.gs, z.f, z.d), f32)],
        [SMEM] + [VMEM] * (z.src + 2) + [HBM, VMEM, VMEM],
        [VMEM] * (2 + z.dp) + [HBM],
        [
            pltpu.VMEM((z.f, z.d), f32),
            pltpu.SemaphoreType.DMA(()),
            pltpu.VMEM((z.gs - done, z.f, z.d), bf16),
            pltpu.SemaphoreType.DMA((z.gs - done,)),
        ],
        limit=15,
        cost=48 * 2**20,
    )
    return res[0], res[1], res[2:-1], res[-1]


def weight_grads(z, copies, rows, jobs, held, after):
    jobs = [job for job in jobs if job[1] < job[2]]
    kinds = sorted({job[0] for job in jobs})
    operands, spans, alias = [], [], {}
    for which in kinds:
        operands += list(rows[which])
    for which in kinds:
        tiles = rows[which][0].shape[2] // 128
        edges = [-(-tiles * p // 4) * 128 for p in range(5)]
        spans.append([(a, b - a) for a, b in zip(edges, edges[1:])])
    old = [held[which] for which in kinds if held[which] is not None]
    at = 1 + len(operands)
    for i, which in enumerate(kinds):
        if held[which] is not None:
            alias[at] = i
            at += 1

    def body(copy_ref, *refs):
        ins = refs[: len(operands)]
        outs = refs[len(operands) + len(old) + 1 :]
        mark = outs[len(kinds)]
        bufs = outs[len(kinds) + 1 : -1]
        sems = outs[-1]
        mark[...] = jnp.zeros_like(mark)

        def copy_of(i, e, p):
            start, size = spans[i][p]
            src = bufs[i].at[pl.ds(start, size), :]
            return pltpu.make_async_copy(src, outs[i].at[e, pl.ds(start, size), :], sems.at[i, p])

        def work(i, first, parts, busy, e, ids):
            left = ins[2 * i]
            r = rows_of(ins[2 * i + 1], ids)
            for p in parts:
                start, size = spans[i][p]
                l = [left[b, :, start : start + size] for b in ids]
                v = dot_tn(l[0] if len(ids) == 1 else jnp.concatenate(l, axis=0), r)
                if (i, p) in busy:
                    copy_of(i, e - 1, p).wait()
                else:

                    @pl.when(e > first)
                    def _():
                        copy_of(i, e - 1, p).wait()

                bufs[i][start : start + size, :] = v
                copy_of(i, e, p).start()

        pending = {}
        for which, first, last, parts in jobs:
            i = kinds.index(which)
            parts = [p for p in parts if spans[i][p][1] > 0]
            busy = frozenset(pending)

            def one(e, ids, i=i, first=first, parts=parts, busy=busy):
                work(i, first, parts, busy, e, ids)

            per_expert(z, copy_ref, one, first, last)
            for p in parts:
                pending[(i, p)] = last - 1
        for (i, p), e in pending.items():
            copy_of(i, e, p).wait()

    outs = [
        pltpu.HBM((z.gs, rows[which][0].shape[2], rows[which][1].shape[2]), f32)
        for which in kinds
    ]
    res = call(
        body,
        (copies, *operands, *old, after),
        outs + [token()],
        [SMEM] + [VMEM] * len(operands) + [HBM] * len(old) + [ANY],
        [HBM] * len(kinds) + [VMEM],
        [pltpu.VMEM((rows[w][0].shape[2], rows[w][1].shape[2]), f32) for w in kinds]
        + [pltpu.SemaphoreType.DMA((len(kinds), 4))],
        limit=24,
        cost=4 * z.f * z.d * sum(job[2] - job[1] for job in jobs),
        aliases=alias,
    )
    held = list(held)
    for i, which in enumerate(kinds):
        held[which] = res[i]
    return held, res[-1]


def pair_sum(z, own, got, after):
    def body(*refs):
        for m in range(z.et):
            total = refs[0][m].astype(f32)
            for c in range(1, z.dp):
                total = total + refs[c][m].astype(f32)
            refs[z.dp + 1 + m][...] = total.astype(bf16)

    return call(
        body,
        (own, *got, after),
        [shape((2 * z.half, z.d), bf16)] * z.et,
        [VMEM] * z.dp + [ANY],
        [VMEM] * z.et,
    )


def to_frames(z, parts, after):
    def body(*refs):
        total = refs[0][...].astype(f32)
        for m in range(1, z.et):
            total = total + refs[m][...].astype(f32)
        frames = dot_tn(block_select(z), total.astype(bf16))
        for k in range(z.ex):
            refs[z.et + 1 + k][...] = frames[k * z.frame : (k + 1) * z.frame].astype(bf16)

    return call(
        body,
        (*parts, after),
        [shape((z.frame, z.d), bf16)] * z.ex,
        [VMEM] * z.et + [ANY],
        [VMEM] * z.ex,
    )


def combine(z, gates, cotangent, tables, frames, after):
    def body(gate_ref, cot_ref, t0, t1, t2, *refs):
        rows = stack_frames(refs[: z.ex])
        layer_ref, gtok_ref, ggate_ref = refs[z.ex + 1 :]
        cot = cot_ref[...].astype(f32)
        p0 = dot_tn(t0[...], rows)
        p1 = dot_tn(t1[...], rows)
        gate0 = as_column(gate_ref[0:1, :])
        gate1 = as_column(gate_ref[1:2, :])
        layer_ref[...] = (gate0 * p0 + gate1 * p1).astype(bf16)
        ggate_ref[0:1, :] = as_row(jnp.sum(cot * p0, axis=1, keepdims=True))
        ggate_ref[1:2, :] = as_row(jnp.sum(cot * p1, axis=1, keepdims=True))
        gtok_ref[...] = dot_tn(t2[...], rows).astype(bf16)

    return call(
        body,
        (gates, cotangent, *tables, *frames, after),
        [shape((z.tok, z.d), bf16), shape((z.tok, z.d), bf16), shape((2, z.tok), f32)],
        [VMEM] * (5 + z.ex) + [ANY],
        [VMEM] * 3,
    )


def shards(tokens, gate_probs, expert_ids, copies, weight_in, weight_out, cotangent):
    z = Sizes(tokens, weight_in, copies)
    gates = gate_probs.T
    frames, tables = send_frame(z, tokens, gates, expert_ids.T, copies, cotangent)
    got = frame_moves(z, frames)
    win, mark = load_weights(weight_in, frames[0], z.gs)
    own_x, own_u = to_blocks(z, got, mark)
    mine_x = plane_moves(z, own_x)
    mine_u = plane_moves(z, own_u)
    wout, mark = load_weights(weight_out, own_x, z.gs // 2)
    blocks_x = swap_cores(z, mine_x, mark)
    xall, pre, hid, mark = forward_in(z, copies, blocks_x, win, wout)
    blocks_u = swap_cores(z, mine_u, mark)
    early = 1
    split = z.gs // 2
    uall, slope, parts, grad_out = middle(
        z, copies, blocks_u, win, wout, weight_out, pre, hid, early
    )
    pairs = ((hid, uall), (xall, slope))
    held = [grad_out, None]
    swapped = [move(parts[c], "dp", z.dp, c) for c in range(1, z.dp)]
    held, mark = weight_grads(z, copies, pairs, [(0, early, early + 1, (0, 1))], held, parts[1])
    sums = pair_sum(z, parts[0], swapped, mark)
    parts = [sums[0]] + [move(sums[m], "et", z.et, m) for m in range(1, z.et)]
    jobs = [
        (0, early, early + 1, (2, 3)),
        (0, early + 1, z.gs, range(4)),
        (1, 0, split, range(4)),
    ]
    held, mark = weight_grads(z, copies, pairs, jobs, held, sums[0])
    frames = to_frames(z, parts, mark)
    frames = frame_moves(z, frames)
    held, mark = weight_grads(z, copies, pairs, [(1, split, z.gs, range(4))], held, frames[0])
    grad_weight_out, grad_weight_in = held
    layer_out, grad_tokens, grad_gates = combine(z, gates, cotangent, tables, frames, mark)
    return (layer_out, grad_tokens, grad_gates.T, grad_weight_in, grad_weight_out)


def solution(mesh):
    rows = P(("et", "ex", "dp"), None)
    w_in = P("ex", None, ("et", "dp"))
    w_out = P("ex", ("et", "dp"), None)
    return jax.shard_map(
        shards,
        mesh=mesh,
        in_specs=(rows, rows, rows, P(), w_in, w_out, rows),
        out_specs=(rows, rows, rows, w_in, w_out),
        check_vma=False,
    )
```

```python
import jax
import jax.numpy as jnp
from jax import lax
from jax.experimental import pallas as pl
from jax.experimental.pallas import tpu as pltpu
from jax.sharding import PartitionSpec as P


gelu_scale = 0.7978845608028654
bf16 = jnp.bfloat16
f32 = jnp.float32

ANY = pl.BlockSpec(memory_space=pl.ANY)
VMEM = pl.BlockSpec(memory_space=pltpu.VMEM)
SMEM = pl.BlockSpec(memory_space=pltpu.SMEM)
HBM = pl.BlockSpec(memory_space=pltpu.HBM)


def dot(a, b):
    return lax.dot_general(a, b, (((1,), (0,)), ((), ())), preferred_element_type=f32)


def dot_nt(a, b):
    return lax.dot_general(a, b, (((1,), (1,)), ((), ())), preferred_element_type=f32)


def dot_tn(a, b):
    return lax.dot_general(a, b, (((0,), (0,)), ((), ())), preferred_element_type=f32)


def gelu_tanh(v):
    return 0.5 * v * (1.0 + jnp.tanh(gelu_scale * (v + 0.044715 * v * v * v)))


def gelu_slope(v):
    t = jnp.tanh(gelu_scale * (v + 0.044715 * v * v * v))
    inner = gelu_scale * (1.0 + 3.0 * 0.044715 * v * v)
    return 0.5 * (1.0 + t) + 0.5 * v * (1.0 - t * t) * inner


def call(body, ins, outs, specs_in, specs_out, scratch=(), limit=8, cost=0, aliases=None):
    ins = [
        v if any(spec is s for s in (ANY, SMEM)) else pltpu.with_memory_space_constraint(v, spec.memory_space)
        for v, spec in zip(ins, specs_in)
    ]
    return pl.pallas_call(
        body,
        in_specs=specs_in,
        out_specs=specs_out,
        out_shape=outs,
        scratch_shapes=list(scratch),
        compiler_params=pltpu.CompilerParams(vmem_limit_bytes=limit * 2**20),
        cost_estimate=pl.CostEstimate(flops=0, transcendentals=0, bytes_accessed=cost or 2**20),
        input_output_aliases=aliases or {},
    )(*ins)


def shape(dims, kind):
    return jax.ShapeDtypeStruct(dims, kind)


def token():
    return shape((8, 128), f32)


def log2(n):
    assert n & (n - 1) == 0
    return n.bit_length() - 1


def move(value, axis, size, offset):
    return lax.ppermute(value, axis, [(i, i ^ offset) for i in range(size)])


class Sizes:
    def __init__(self, tokens, weight_in, copies):
        self.et = lax.axis_size("et")
        self.ex = lax.axis_size("ex")
        self.dp = lax.axis_size("dp")
        self.tok, self.d = tokens.shape
        self.experts = copies.shape[0]
        self.gs = self.experts // self.ex
        self.f = weight_in.shape[2]
        self.cap = max(2, self.tok // 16)
        self.nb = self.gs + 1
        self.slots = self.nb * self.cap
        self.frame = -(-2 * self.slots // 8) * 8
        self.rb = self.ex * self.cap
        self.half = self.nb * self.rb
        self.src = self.et * self.dp
        self.rows = self.src * self.rb


def diagonal(n):
    row = lax.broadcasted_iota(jnp.int32, (n, n), 0)
    return row == lax.broadcasted_iota(jnp.int32, (n, n), 1)


def as_column(row):
    return jnp.sum(jnp.where(diagonal(row.shape[1]), row, 0.0), axis=1, keepdims=True)


def as_row(column):
    return jnp.sum(jnp.where(diagonal(column.shape[0]), column, 0.0), axis=0, keepdims=True)


def stack_frames(refs):
    return jnp.concatenate([r[...].astype(f32) for r in refs], axis=0).astype(bf16)


def send_frame(z, tokens, gates, ids, copies, cotangent):
    ins = (tokens, gates, ids, copies.reshape(1, -1), cotangent)

    def body(*refs):
        n = len(ins)
        outs, held, sem = refs[n : n + z.ex + 3], refs[n + z.ex + 3 : -1], refs[-1]
        fetch = [pltpu.make_async_copy(refs[i], held[i], sem.at[i]) for i in range(n)]
        for c in fetch:
            c.start()
        for c in fetch:
            c.wait()
        tok_ref, gate_ref, id_ref, copy_ref, cot_ref = held
        me = lax.axis_index("ex")
        lab = lax.broadcasted_iota(jnp.int32, (z.experts, z.tok), 0)
        hot = [id_ref[k : k + 1, :] == lab for k in range(2)]
        count = (hot[0].astype(f32) + hot[1].astype(f32)).astype(bf16)
        row = lax.broadcasted_iota(jnp.int32, (z.tok, z.tok), 0)
        col = lax.broadcasted_iota(jnp.int32, (z.tok, z.tok), 1)
        earlier = dot(count, (row < col).astype(f32).astype(bf16))
        allow = as_column((copy_ref[...] * z.cap).astype(f32))
        places = lax.broadcasted_iota(jnp.int32, (z.ex * z.frame, z.tok), 0)
        in_tables, up_tables, ups = [], [], []
        cot = cot_ref[...].astype(f32)
        for k in range(2):
            rank = jnp.sum(jnp.where(hot[k], earlier, 0.0), axis=0, keepdims=True)
            limit = jnp.sum(jnp.where(hot[k], allow, 0.0), axis=0, keepdims=True)
            irank = rank.astype(jnp.int32)
            eid = id_ref[k : k + 1, :]
            group = (eid >> log2(z.gs)) ^ me
            within = eid & (z.gs - 1)
            slot = jnp.where(irank < z.cap, within * z.cap, (z.gs - 1) * z.cap) + irank
            target = group * z.frame + slot
            kept = rank < limit
            in_tables.append((jnp.where(kept, target, -1) == places).astype(f32).astype(bf16))
            up_tables.append(
                (jnp.where(kept, target + z.slots, -1) == places).astype(f32).astype(bf16)
            )
            ups.append((as_column(gate_ref[k : k + 1, :]) * cot).astype(bf16))
        sent = dot(in_tables[0] + in_tables[1], tok_ref[...])
        sent = sent + (dot(up_tables[0], ups[0]) + dot(up_tables[1], ups[1]))
        for k in range(z.ex):
            outs[k][...] = sent[k * z.frame : (k + 1) * z.frame].astype(bf16)
        outs[z.ex][...] = in_tables[0]
        outs[z.ex + 1][...] = in_tables[1]
        outs[z.ex + 2][...] = up_tables[0] + up_tables[1]

    outs = [shape((z.frame, z.d), bf16)] * z.ex + [shape((z.ex * z.frame, z.tok), bf16)] * 3
    res = call(
        body,
        ins,
        outs,
        [HBM] * len(ins),
        [VMEM] * len(outs),
        [pltpu.VMEM(v.shape, v.dtype) for v in ins] + [pltpu.SemaphoreType.DMA((len(ins),))],
    )
    return res[: z.ex], res[z.ex :]


def block_select(z):
    dims = (2 * z.half, z.ex * z.frame)
    r = lax.broadcasted_iota(jnp.int32, dims, 0)
    c = lax.broadcasted_iota(jnp.int32, dims, 1)
    upper = r >= z.half
    r = jnp.where(upper, r - z.half, r)
    block = r >> log2(z.rb)
    source = (r & (z.rb - 1)) >> log2(z.cap)
    slot = r & (z.cap - 1)
    want = source * z.frame + block * z.cap + slot + jnp.where(upper, z.slots, 0)
    return (want == c).astype(f32).astype(bf16)


def frame_moves(z, frames):
    moved = []
    for k in range(1, z.ex):
        moved.append(move(frames[k], "ex", z.ex, k))
    return [frames[0]] + moved


def to_blocks(z, frames, after):
    def body(*refs):
        rows = dot(block_select(z), stack_frames(refs[: z.ex]))
        refs[z.ex + 1][...] = rows[: z.half].astype(bf16)
        refs[z.ex + 2][...] = rows[z.half :].astype(bf16)

    return call(
        body, (*frames, after), [shape((z.half, z.d), bf16)] * 2, [VMEM] * z.ex + [ANY], [VMEM] * 2
    )


def load_weights(weight, after, n):
    dims = (n,) + weight.shape[1:]

    def body(w, _, out, mark, sem):
        copies = [pltpu.make_async_copy(w.at[e], out.at[e], sem.at[e]) for e in range(n)]
        for c in copies:
            c.start()
        mark[...] = jnp.zeros_like(mark)
        for c in copies:
            c.wait()

    return call(
        body,
        (weight, after),
        [shape(dims, weight.dtype), token()],
        [HBM, ANY],
        [VMEM, VMEM],
        [pltpu.SemaphoreType.DMA((n,))],
        cost=2 * weight.size // weight.shape[0] * n,
    )


def plane_moves(z, own):
    return [own] + [move(own, "et", z.et, m) for m in range(1, z.et)]


def swap_cores(z, mine, after):
    late, _ = lax.optimization_barrier((mine[1:], after))
    mine = [mine[0]] + late
    others = []
    for c in range(1, z.dp):
        others.append(move(mine[0], "dp", z.dp, c))
        others += [move(v, "dp", z.dp, c) for v in mine[1:]]
    return mine + others


def assemble(z, refs, out):
    for j in range(z.nb):
        out[j] = jnp.concatenate([r[j * z.rb : (j + 1) * z.rb, :] for r in refs], axis=0)


def scatter_rows(z, value, block, base, refs):
    start = pl.multiple_of(base + block * z.rb, 8)
    for i in range(z.src):
        refs[i // z.et][i % z.et, pl.ds(start, z.rb), :] = value[i * z.rb : (i + 1) * z.rb]


def per_expert(z, copy_ref, work, first=0, last=None):
    base = lax.axis_index("ex") * z.gs

    def step(e, carry):
        doubled = copy_ref[base + e] > 1

        @pl.when(doubled)
        def _():
            work(e, (e, z.gs))

        @pl.when(jnp.logical_not(doubled))
        def _():
            work(e, (e,))

        return carry

    lax.fori_loop(first, z.gs if last is None else last, step, 0)


def rows_of(ref, blocks):
    if len(blocks) == 1:
        return ref[blocks[0]]
    return jnp.concatenate([ref[b] for b in blocks], axis=0)


def forward_in(z, copies, blocks, weight_in, after):
    def body(copy_ref, *refs):
        srcs = refs[: z.src]
        w, _, xall, pre, hid, mark = refs[z.src :]
        mark[...] = jnp.zeros_like(mark)
        assemble(z, srcs, xall)

        def work(e, ids):
            v = dot(rows_of(xall, ids), w[e])
            h = gelu_tanh(v).astype(bf16)
            for i, b in enumerate(ids):
                pre[b] = v[i * z.rows : (i + 1) * z.rows]
                hid[b] = h[i * z.rows : (i + 1) * z.rows]

        per_expert(z, copy_ref, work)

    return call(
        body,
        (copies, *blocks, weight_in, after),
        [
            shape((z.nb, z.rows, z.d), bf16),
            shape((z.nb, z.rows, z.f), f32),
            shape((z.nb, z.rows, z.f), bf16),
            token(),
        ],
        [SMEM] + [VMEM] * (z.src + 2),
        [VMEM] * 4,
        cost=16 * 2**20,
    )


def early_out(z, copies, ready, hid):
    def body(copy_ref, w, hid_ref, out):
        def work(e, ids):
            o = dot(rows_of(hid_ref, ids), w[e]).astype(bf16)
            for i, b in enumerate(ids):
                out[b] = o[i * z.rows : (i + 1) * z.rows]

        per_expert(z, copy_ref, work, 0, ready.shape[0])

    return call(
        body,
        (copies, ready, hid),
        shape((z.nb, z.rows, z.d), bf16),
        [SMEM, VMEM, VMEM],
        VMEM,
        cost=8 * 2**20,
    )


def middle(z, copies, blocks, weight_in, ready, weight_out, pre, hid, made, early):
    done = ready.shape[0]

    def body(copy_ref, *refs):
        srcs = refs[: z.src]
        win, wout, whbm, pre_ref, hid_ref, made_ref, uall, slope, *outs = refs[z.src :]
        *outs, grad, buf, sem, wrest, wsem = outs
        fetch = [
            pltpu.make_async_copy(whbm.at[e], wrest.at[e - done], wsem.at[e - done])
            for e in range(done, z.gs)
        ]
        for c in fetch:
            c.start()
        assemble(z, srcs, uall)

        def write(e):
            return pltpu.make_async_copy(buf, grad.at[e], sem)

        def work(e, ids, last=False):
            w = wrest[e - done] if last else wout[e]
            back = dot_nt(rows_of(uall, ids), w)
            s = (back * gelu_slope(rows_of(pre_ref, ids))).astype(bf16)
            if last:
                o = dot(rows_of(hid_ref, ids), w).astype(bf16)
            else:
                o = rows_of(made_ref, ids)
            g = dot_nt(s, win[e]).astype(bf16)
            for i, b in enumerate(ids):
                part = slice(i * z.rows, (i + 1) * z.rows)
                slope[b] = s[part]
                scatter_rows(z, o[part], b, 0, outs)
                scatter_rows(z, g[part], b, z.half, outs)

        def early_work(e, ids):
            work(e, ids)

            @pl.when(e > 0)
            def _():
                write(e - 1).wait()

            r = rows_of(uall, ids)
            for i in range(z.f // 128):
                part = slice(i * 128, (i + 1) * 128)
                l = [hid_ref[b, :, part] for b in ids]
                buf[part, :] = dot_tn(l[0] if len(ids) == 1 else jnp.concatenate(l, axis=0), r)
            write(e).start()

        per_expert(z, copy_ref, early_work, 0, early)
        per_expert(z, copy_ref, work, early, done)
        for c in fetch:
            c.wait()
        per_expert(z, copy_ref, lambda e, ids: work(e, ids, True), done, z.gs)
        write(early - 1).wait()

    res = call(
        body,
        (copies, *blocks, weight_in, ready, weight_out, pre, hid, made),
        [shape((z.nb, z.rows, z.d), bf16), shape((z.nb, z.rows, z.f), bf16)]
        + [shape((z.et, 2 * z.half, z.d), bf16)] * z.dp
        + [pltpu.HBM((z.gs, z.f, z.d), f32)],
        [SMEM] + [VMEM] * (z.src + 2) + [HBM, VMEM, VMEM, VMEM],
        [VMEM] * (2 + z.dp) + [HBM],
        [
            pltpu.VMEM((z.f, z.d), f32),
            pltpu.SemaphoreType.DMA(()),
            pltpu.VMEM((z.gs - done, z.f, z.d), bf16),
            pltpu.SemaphoreType.DMA((z.gs - done,)),
        ],
        limit=15,
        cost=48 * 2**20,
    )
    return res[0], res[1], res[2:-1], res[-1]


def weight_grads(z, copies, rows, jobs, held, after):
    jobs = [job for job in jobs if job[1] < job[2]]
    kinds = sorted({job[0] for job in jobs})
    operands, spans, alias = [], [], {}
    for which in kinds:
        operands += list(rows[which])
    for which in kinds:
        tiles = rows[which][0].shape[2] // 128
        edges = [-(-tiles * p // 4) * 128 for p in range(5)]
        spans.append([(a, b - a) for a, b in zip(edges, edges[1:])])
    old = [held[which] for which in kinds if held[which] is not None]
    at = 1 + len(operands)
    for i, which in enumerate(kinds):
        if held[which] is not None:
            alias[at] = i
            at += 1

    def body(copy_ref, *refs):
        ins = refs[: len(operands)]
        outs = refs[len(operands) + len(old) + 1 :]
        mark = outs[len(kinds)]
        bufs = outs[len(kinds) + 1 : -1]
        sems = outs[-1]
        mark[...] = jnp.zeros_like(mark)

        def copy_of(i, e, p):
            start, size = spans[i][p]
            src = bufs[i].at[pl.ds(start, size), :]
            return pltpu.make_async_copy(src, outs[i].at[e, pl.ds(start, size), :], sems.at[i, p])

        def work(i, first, parts, busy, e, ids):
            left = ins[2 * i]
            r = rows_of(ins[2 * i + 1], ids)
            for p in parts:
                start, size = spans[i][p]
                l = [left[b, :, start : start + size] for b in ids]
                v = dot_tn(l[0] if len(ids) == 1 else jnp.concatenate(l, axis=0), r)
                if (i, p) in busy:
                    copy_of(i, e - 1, p).wait()
                else:

                    @pl.when(e > first)
                    def _():
                        copy_of(i, e - 1, p).wait()

                bufs[i][start : start + size, :] = v
                copy_of(i, e, p).start()

        pending = {}
        for which, first, last, parts in jobs:
            i = kinds.index(which)
            parts = [p for p in parts if spans[i][p][1] > 0]
            busy = frozenset(pending)

            def one(e, ids, i=i, first=first, parts=parts, busy=busy):
                work(i, first, parts, busy, e, ids)

            per_expert(z, copy_ref, one, first, last)
            for p in parts:
                pending[(i, p)] = last - 1
        for (i, p), e in pending.items():
            copy_of(i, e, p).wait()

    outs = [
        pltpu.HBM((z.gs, rows[which][0].shape[2], rows[which][1].shape[2]), f32)
        for which in kinds
    ]
    res = call(
        body,
        (copies, *operands, *old, after),
        outs + [token()],
        [SMEM] + [VMEM] * len(operands) + [HBM] * len(old) + [ANY],
        [HBM] * len(kinds) + [VMEM],
        [pltpu.VMEM((rows[w][0].shape[2], rows[w][1].shape[2]), f32) for w in kinds]
        + [pltpu.SemaphoreType.DMA((len(kinds), 4))],
        limit=24,
        cost=4 * z.f * z.d * sum(job[2] - job[1] for job in jobs),
        aliases=alias,
    )
    held = list(held)
    for i, which in enumerate(kinds):
        held[which] = res[i]
    return held, res[-1]


def pair_sum(z, own, got, after):
    def body(*refs):
        for m in range(z.et):
            total = refs[0][m].astype(f32)
            for c in range(1, z.dp):
                total = total + refs[c][m].astype(f32)
            refs[z.dp + 1 + m][...] = total.astype(bf16)

    return call(
        body,
        (own, *got, after),
        [shape((2 * z.half, z.d), bf16)] * z.et,
        [VMEM] * z.dp + [ANY],
        [VMEM] * z.et,
    )


def to_frames(z, parts, after):
    def body(*refs):
        total = refs[0][...].astype(f32)
        for m in range(1, z.et):
            total = total + refs[m][...].astype(f32)
        frames = dot_tn(block_select(z), total.astype(bf16))
        for k in range(z.ex):
            refs[z.et + 1 + k][...] = frames[k * z.frame : (k + 1) * z.frame].astype(bf16)

    return call(
        body,
        (*parts, after),
        [shape((z.frame, z.d), bf16)] * z.ex,
        [VMEM] * z.et + [ANY],
        [VMEM] * z.ex,
    )


def combine(z, gates, cotangent, tables, frames, after):
    def body(gate_ref, cot_ref, t0, t1, t2, *refs):
        rows = stack_frames(refs[: z.ex])
        layer_ref, gtok_ref, ggate_ref = refs[z.ex + 1 :]
        cot = cot_ref[...].astype(f32)
        p0 = dot_tn(t0[...], rows)
        p1 = dot_tn(t1[...], rows)
        gate0 = as_column(gate_ref[0:1, :])
        gate1 = as_column(gate_ref[1:2, :])
        layer_ref[...] = (gate0 * p0 + gate1 * p1).astype(bf16)
        ggate_ref[0:1, :] = as_row(jnp.sum(cot * p0, axis=1, keepdims=True))
        ggate_ref[1:2, :] = as_row(jnp.sum(cot * p1, axis=1, keepdims=True))
        gtok_ref[...] = dot_tn(t2[...], rows).astype(bf16)

    return call(
        body,
        (gates, cotangent, *tables, *frames, after),
        [shape((z.tok, z.d), bf16), shape((z.tok, z.d), bf16), shape((2, z.tok), f32)],
        [VMEM] * (5 + z.ex) + [ANY],
        [VMEM] * 3,
    )


def shards(tokens, gate_probs, expert_ids, copies, weight_in, weight_out, cotangent):
    z = Sizes(tokens, weight_in, copies)
    gates = gate_probs.T
    frames, tables = send_frame(z, tokens, gates, expert_ids.T, copies, cotangent)
    got = frame_moves(z, frames)
    win, mark = load_weights(weight_in, frames[0], z.gs)
    own_x, own_u = to_blocks(z, got, mark)
    mine_x = plane_moves(z, own_x)
    mine_u = plane_moves(z, own_u)
    wout, mark = load_weights(weight_out, own_x, z.gs // 2)
    blocks_x = swap_cores(z, mine_x, mark)
    xall, pre, hid, mark = forward_in(z, copies, blocks_x, win, wout)
    blocks_u = swap_cores(z, mine_u, mark)
    made = early_out(z, copies, wout, hid)
    early = 1
    split = z.gs // 2
    uall, slope, parts, grad_out = middle(
        z, copies, blocks_u, win, wout, weight_out, pre, hid, made, early
    )
    pairs = ((hid, uall), (xall, slope))
    held = [grad_out, None]
    swapped = [move(parts[c], "dp", z.dp, c) for c in range(1, z.dp)]
    held, mark = weight_grads(z, copies, pairs, [(0, early, early + 1, (0, 1))], held, parts[1])
    sums = pair_sum(z, parts[0], swapped, mark)
    parts = [sums[0]]
    for m in range(1, z.et):
        parts.append(move(sums[m], "et", z.et, m))
    jobs = [
        (0, early, early + 1, (2, 3)),
        (0, early + 1, z.gs, range(4)),
        (1, 0, split, range(4)),
    ]
    held, mark = weight_grads(z, copies, pairs, jobs, held, sums[0])
    frames = to_frames(z, parts, mark)
    frames = frame_moves(z, frames)
    held, mark = weight_grads(z, copies, pairs, [(1, split, z.gs, range(4))], held, frames[0])
    grad_weight_out, grad_weight_in = held
    layer_out, grad_tokens, grad_gates = combine(z, gates, cotangent, tables, frames, mark)
    return (layer_out, grad_tokens, grad_gates.T, grad_weight_in, grad_weight_out)


def solution(mesh):
    rows = P(("et", "ex", "dp"), None)
    w_in = P("ex", None, ("et", "dp"))
    w_out = P("ex", ("et", "dp"), None)
    return jax.shard_map(
        shards,
        mesh=mesh,
        in_specs=(rows, rows, rows, P(), w_in, w_out, rows),
        out_specs=(rows, rows, rows, w_in, w_out),
        check_vma=False,
    )
```
